256 devices in a mesh: inp: 32 (over y, z_hi, core), tm: 8 (over z_lo, x).
Axes of the slice: x: 4, y: 4, z: 8 (z_hi: 4, z_lo: 2; z = z_hi * 2 + z_lo), core: 2. Of those that a mesh axis runs over, the one named last changes fastest.
Arguments:
- voltages: bfloat16 [512, 524288], P('inp', 'tm'), may hold values from -6 to 6
- taps: float32 [4, 512], replicated, may hold values from -3 to 3
Outputs:
- visibility: float32 [256, 2, 512, 512], P(('inp', 'tm'))
The draws below stay inside these ranges and needn't reach their ends.
All inputs are finite; a program needn't handle non-finite values.
Results may differ from the reference program's by a relative error of at most 0.0038.
Values may be sent and summed in bfloat16 or wider, within the bound.
A program may use at most 128 MiB of HBM per device.

```python
import math
import jax
import jax.numpy as jnp
from jax import lax

INPUTS = 512
CH = 256
TAPS = 4
SPECTRA = 1024
SAMPLES = 524288


def shard_levels(own_key, extent, shards, low, largest):
    def one(dim, blocks):
        draws = jax.random.uniform(jax.random.fold_in(jax.random.fold_in(own_key, 6), dim), (blocks,), jnp.float32, low / len(shards), largest / len(shards))
        return jnp.repeat(jnp.exp(draws), extent[dim] // blocks).reshape((-1,) + (1,) * (len(extent) - dim - 1))

    level = one(*shards[0])
    for cut in shards[1:]:
        level = level * one(*cut)
    return level


def centred(stream_key, shape, deviation, reach, shards=(), held_as=jnp.bfloat16):
    gain = shard_levels(stream_key, shape, shards, -0.22, 0.18) if shards else 1.0
    result = jax.random.normal(stream_key, shape, jnp.float32) * deviation * gain
    return jnp.minimum(jnp.maximum(result, -reach), reach).astype(held_as)


def setup_inputs(seed: int = 0) -> dict:
    streams_of = jax.random.split(jax.random.key(seed), 3)
    return {
        "voltages": centred(streams_of[0], (INPUTS, SAMPLES), 1.0, 6.0, ((0, 32), (1, 8))),
        "taps": centred(streams_of[1], (TAPS, 2 * CH), 0.5, 3.0, (), jnp.float32),
    }


def dft_tables(width, channels):
    sample_idx = jnp.arange(width, dtype=jnp.int32)
    chan_idx = jnp.arange(channels, dtype=jnp.int32)
    phase = (sample_idx[:, None] * chan_idx[None, :]) % width
    angle = phase.astype(jnp.float32) * (2.0 * math.pi / width)
    return jnp.cos(angle).astype(jnp.bfloat16), (-jnp.sin(angle)).astype(jnp.bfloat16)


def reference(voltages, taps):
    width = 2 * CH
    blocks = voltages.reshape(INPUTS, SPECTRA, width)
    padded = jnp.concatenate([jnp.zeros((INPUTS, TAPS - 1, width), voltages.dtype), blocks], axis=1)
    filtered = jnp.zeros((INPUTS, SPECTRA, width), jnp.float32)
    for tap in range(TAPS):
        filtered = filtered + taps[tap][None, None, :] * padded[:, tap:tap + SPECTRA, :].astype(jnp.float32)
    filtered = filtered.astype(jnp.bfloat16)
    cos_table, sin_table = dft_tables(width, CH)
    spec_real = jnp.einsum("isn,nk->kis", filtered.astype(jnp.float32), cos_table.astype(jnp.float32)).astype(jnp.bfloat16)
    spec_imag = jnp.einsum("isn,nk->kis", filtered.astype(jnp.float32), sin_table.astype(jnp.float32)).astype(jnp.bfloat16)
    scale = 1.0 / (SPECTRA * width)

    def one_channel(pair):
        real_part, imag_part = pair
        cross_real = jnp.dot(real_part, real_part.T, preferred_element_type=jnp.float32) + jnp.dot(imag_part, imag_part.T, preferred_element_type=jnp.float32)
        cross_imag = jnp.dot(imag_part, real_part.T, preferred_element_type=jnp.float32) - jnp.dot(real_part, imag_part.T, preferred_element_type=jnp.float32)
        return jnp.stack([cross_real * scale, cross_imag * scale], axis=0)

    return lax.map(one_channel, (spec_real, spec_imag))
```

```python
import functools
import math

import jax
import jax.numpy as jnp
import ml_dtypes
import numpy as np
from jax import lax
from jax.experimental import pallas as pl
from jax.experimental.pallas import tpu as pltpu
from jax.sharding import PartitionSpec as P

MESH = pl.DeviceIdType.MESH
NX, NY, NZ, NC, ZL = 4, 4, 8, 2, 2
ZH = NZ // ZL
PLANE = NY * NX * NC
HALF = 8
LANES = 128


def position():
    inp = lax.axis_index("inp")
    tm = lax.axis_index("tm")
    return tm % NX, inp // (ZH * NC), (inp // NC) % ZH * ZL + tm // NX, inp % NC


def device(x, y, z, c):
    return (y * ZH + z // ZL) * NC + c, (z % ZL) * NX + x


def channel_of_row():
    order = np.empty((NY, NX, NC, NZ), np.int64)
    for y in range(NY):
        for x in range(NX):
            for c in range(NC):
                for z in range(NZ):
                    inp, tm = device(x, y, z, c)
                    order[y, x, c, z] = inp * (ZL * NX) + tm
    return order.reshape(-1)


def dft_rows(width):
    channel = channel_of_row()
    phase = (channel[:, None] * np.arange(width)[None, :]) % width
    angle = phase.astype(np.float32) * np.float32(2.0 * math.pi / width)
    rows = np.concatenate([np.cos(angle), -np.sin(angle)], axis=0)
    return rows.astype(ml_dtypes.bfloat16)


def exchange_kernel(
    v_hbm, taps_ref, table_ref, r_ref,
    v, hist, f32s, s32, sa, sb, za, yb,
    load_sem, hist_send, hist_recv, local_sem,
    za_send, za_recv, xa_send, xa_recv, xb_send, xb_recv, zb_send, zb_recv,
):
    x, y, z, c = position()
    zh, zl = z // ZL, z % ZL
    tm = lax.axis_index("tm")
    inp = lax.axis_index("inp")
    tms = ZL * NX
    width = taps_ref.shape[1]
    spectra = v.shape[1] // width
    rows = v.shape[0]
    taps_n = taps_ref.shape[0]

    load = pltpu.make_async_copy(v_hbm, v, load_sem)
    load.start()

    def z_peer(dz):
        zz = (z + dz) % NZ
        return zz, device(x, y, zz, c)

    def plane_peer(i):
        xx = (x + i // (NY * NC)) % NX
        yy = (y + (i // NC) % NY) % NY
        cc = (c + i % NC) % NC
        return xx, yy, cc, device(xx, yy, z, cc)

    later = (inp, (tm + 1) % tms)
    earlier = (inp, (tm + tms - 1) % tms)
    barrier = pltpu.get_barrier_semaphore()
    pl.semaphore_signal(barrier, inc=1, device_id=later, device_id_type=MESH)
    pl.semaphore_signal(barrier, inc=1, device_id=earlier, device_id_type=MESH)
    for dz in range(1, NZ):
        pl.semaphore_signal(barrier, inc=1, device_id=z_peer(dz)[1], device_id_type=MESH)

    def greet(i, _):
        pl.semaphore_signal(barrier, inc=1, device_id=plane_peer(i)[3], device_id_type=MESH)
        return 0

    lax.fori_loop(1, PLANE, greet, 0)
    pl.semaphore_wait(barrier, 2 + NZ - 1 + PLANE - 1)

    history = pltpu.make_async_remote_copy(
        src_ref=v_hbm.at[:, pl.ds((spectra - (taps_n - 1)) * width, (taps_n - 1) * width)],
        dst_ref=hist,
        send_sem=hist_send,
        recv_sem=hist_recv,
        device_id=later,
        device_id_type=MESH,
    )
    history.start()
    load.wait()

    gains = [
        jnp.broadcast_to(taps_ref[t : t + 1, :], (rows, width)) for t in range(taps_n)
    ]

    def block(ref, s):
        return ref[:, pl.ds(pl.multiple_of(s * width, width), width)].astype(jnp.float32)

    def weigh(past):
        total = gains[0] * past[0]
        for t in range(1, taps_n):
            total = total + gains[t] * past[t]
        return total

    def put(s, value):
        for q in range(width // LANES):
            f32s.at[q][pl.ds(s, rows, stride=spectra), :] = value[:, q * LANES : (q + 1) * LANES]

    def step(s, past):
        past = past + (block(v, s),)
        put(s, weigh(past))
        return past[1:]

    first = tuple(block(v, s) for s in range(taps_n - 1))
    lax.fori_loop(taps_n - 1, spectra, step, first)

    history.wait()
    seen = tm > 0
    past = tuple(
        jnp.where(seen, block(hist, s), 0.0) for s in range(taps_n - 1)
    )
    for s in range(taps_n - 1):
        past = step(s, past)

    def transform(half, out):
        def pair(p, _):
            i = half * HALF + 2 * p
            at = pl.ds(pl.multiple_of(i * spectra, LANES), 2 * spectra)
            f = jnp.concatenate(
                [f32s[q, at, :] for q in range(width // LANES)], axis=1
            ).astype(jnp.bfloat16)
            spec = lax.dot_general(
                table_ref[...], f, (((1,), (1,)), ((), ())), preferred_element_type=jnp.float32
            )
            for two in range(2):
                for plane in range(2):
                    s32.at[plane][pl.ds(2 * p + two, width // 2, stride=HALF), :] = spec[
                        plane * (width // 2) : (plane + 1) * (width // 2),
                        two * spectra : (two + 1) * spectra,
                    ]
            return 0

        lax.fori_loop(0, HALF // 2, pair, 0)

        def pack(m, _):
            at = pl.ds(pl.multiple_of(m * NZ * HALF, NZ * HALF), NZ * HALF)
            both = jnp.concatenate([s32[0, at, :], s32[1, at, :]], axis=1)
            out[m] = both.reshape(NZ, HALF, 2 * spectra).astype(jnp.bfloat16)
            return 0

        lax.fori_loop(0, PLANE, pack, 0)

    here = (y * NX + x) * NC + c

    transform(0, sa)

    def za_copy(dz):
        zz, peer = z_peer(dz)
        return pltpu.make_async_remote_copy(
            src_ref=sa.at[:, zz],
            dst_ref=za.at[zl, zh],
            send_sem=za_send.at[dz - 1],
            recv_sem=za_recv.at[dz - 1],
            device_id=peer,
            device_id_type=MESH,
        )

    for dz in (4, 3, 5, 2, 6, 1, 7):
        za_copy(dz).start()
    keep_a = pltpu.make_async_copy(sa.at[:, z], za.at[zl, zh], local_sem.at[0])
    keep_a.start()

    transform(1, sb)

    def xb_copy(i):
        xx, yy, cc, peer = plane_peer(i)
        return pltpu.make_async_remote_copy(
            src_ref=sb.at[(yy * NX + xx) * NC + cc],
            dst_ref=yb.at[x, y, c],
            send_sem=xb_send.at[i - 1],
            recv_sem=xb_recv.at[i - 1],
            device_id=peer,
            device_id_type=MESH,
        )

    def xb_start(i, _):
        xb_copy(i).start()
        return 0

    lax.fori_loop(1, PLANE, xb_start, 0)
    keep_b = pltpu.make_async_copy(sb.at[here], yb.at[x, y, c], local_sem.at[1])
    keep_b.start()

    def xb_wait(i, _):
        xb_copy(i).wait()
        return 0

    lax.fori_loop(1, PLANE, xb_wait, 0)
    keep_b.wait()

    def zb_copy(dz):
        zz, peer = z_peer(dz)
        return pltpu.make_async_remote_copy(
            src_ref=yb.at[:, :, :, zz],
            dst_ref=r_ref.at[zl, :, :, zh, :, 1],
            send_sem=zb_send.at[dz - 1],
            recv_sem=zb_recv.at[dz - 1],
            device_id=peer,
            device_id_type=MESH,
        )

    for dz in (4, 3, 5, 2, 6, 1, 7):
        zb_copy(dz).start()
    last_b = pltpu.make_async_copy(
        yb.at[:, :, :, z], r_ref.at[zl, :, :, zh, :, 1], local_sem.at[2]
    )
    last_b.start()

    for dz in range(1, NZ):
        za_copy(dz).wait()
    keep_a.wait()

    def xa_copy(i):
        xx, yy, cc, peer = plane_peer(i)
        return pltpu.make_async_remote_copy(
            src_ref=za.at[:, :, (yy * NX + xx) * NC + cc],
            dst_ref=r_ref.at[:, x, y, :, c, 0],
            send_sem=xa_send.at[i - 1],
            recv_sem=xa_recv.at[i - 1],
            device_id=peer,
            device_id_type=MESH,
        )

    def xa_start(i, _):
        xa_copy(i).start()
        return 0

    lax.fori_loop(1, PLANE, xa_start, 0)
    last_a = pltpu.make_async_copy(
        za.at[:, :, here], r_ref.at[:, x, y, :, c, 0], local_sem.at[3]
    )
    last_a.start()

    def xa_wait(i, _):
        xa_copy(i).wait()
        return 0

    lax.fori_loop(1, PLANE, xa_wait, 0)
    last_a.wait()
    for dz in range(1, NZ):
        zb_copy(dz).wait()
    last_b.wait()


def exchange(voltages, taps, table):
    inp_dev, samples = voltages.shape
    width = taps.shape[1]
    spectra = samples // width
    block = (HALF, 2 * spectra)
    bf16 = jnp.bfloat16
    dma = pltpu.SemaphoreType.DMA
    return pl.pallas_call(
        exchange_kernel,
        name="exchange",
        out_shape=jax.ShapeDtypeStruct((ZL, NX, NY, ZH, NC, inp_dev // HALF) + block, bf16),
        in_specs=[
            pl.BlockSpec(memory_space=pl.ANY),
            pl.BlockSpec(memory_space=pltpu.VMEM),
            pl.BlockSpec(memory_space=pltpu.VMEM),
        ],
        out_specs=pl.BlockSpec(memory_space=pltpu.VMEM),
        scratch_shapes=[
            pltpu.VMEM((inp_dev, samples), bf16),
            pltpu.VMEM((inp_dev, (taps.shape[0] - 1) * width), bf16),
            pltpu.VMEM((width // LANES, inp_dev * spectra, LANES), jnp.float32),
            pltpu.VMEM((2, width // 2 * HALF, spectra), jnp.float32),
            pltpu.VMEM((PLANE, NZ) + block, bf16),
            pltpu.VMEM((PLANE, NZ) + block, bf16),
            pltpu.VMEM((ZL, ZH, PLANE) + block, bf16),
            pltpu.VMEM((NX, NY, NC, NZ) + block, bf16),
            dma(()), dma(()), dma(()), dma((4,)),
            dma((NZ - 1,)), dma((NZ - 1,)),
            dma((PLANE - 1,)), dma((PLANE - 1,)),
            dma((PLANE - 1,)), dma((PLANE - 1,)),
            dma((NZ - 1,)), dma((NZ - 1,)),
        ],
        compiler_params=pltpu.CompilerParams(
            collective_id=0, has_side_effects=True, vmem_limit_bytes=48 << 20
        ),
    )(voltages, taps, table)


def correlate_kernel(scale, r_ref, o_ref):
    m = pl.program_id(0)
    size = o_ref.shape[2]
    times = r_ref.shape[0]
    half = r_ref.shape[2] // 2
    real = jnp.zeros(o_ref.shape[2:], jnp.float32)
    imag = jnp.zeros(o_ref.shape[2:], jnp.float32)
    contract = (((1,), (1,)), ((), ()))
    at = pl.ds(pl.multiple_of(m * size, size), size)
    for t in range(times):
        mine = r_ref[t, at, :]
        turned = jnp.concatenate([mine[:, half:], -mine[:, :half]], axis=1)
        every = r_ref[t]
        real += lax.dot_general(mine, every, contract, preferred_element_type=jnp.float32)
        imag += lax.dot_general(turned, every, contract, preferred_element_type=jnp.float32)
    o_ref[0, 0] = real * scale
    o_ref[0, 1] = imag * scale


def correlate(spectra, scale, size=128):
    inputs = spectra.shape[1]
    return pl.pallas_call(
        functools.partial(correlate_kernel, scale),
        name="correlate",
        grid=(inputs // size,),
        out_shape=jax.ShapeDtypeStruct((1, 2, inputs, inputs), jnp.float32),
        in_specs=[pl.BlockSpec(memory_space=pltpu.VMEM)],
        out_specs=pl.BlockSpec((1, 2, size, inputs), lambda m: (0, 0, m, 0)),
        compiler_params=pltpu.CompilerParams(vmem_limit_bytes=32 << 20),
    )(spectra)


def local(voltages, taps):
    width = taps.shape[1]
    table = jnp.asarray(dft_rows(width))
    times = lax.axis_size("tm")
    spectra = voltages.shape[1] // width
    scale = 1.0 / (spectra * times * width)
    gathered = exchange(voltages, taps, table)
    return correlate(gathered.reshape(times, -1, 2 * spectra), scale)


def solution(mesh):
    in_specs = (P("inp", "tm"), P())
    out_specs = P(("inp", "tm"), None, None, None)
    return jax.shard_map(local, mesh=mesh, in_specs=in_specs, out_specs=out_specs, check_vma=False)
```

```python
import functools
import math

import jax
import jax.numpy as jnp
import ml_dtypes
import numpy as np
from jax import lax
from jax.experimental import pallas as pl
from jax.experimental.pallas import tpu as pltpu
from jax.sharding import PartitionSpec as P

MESH = pl.DeviceIdType.MESH
NX, NY, NZ, NC, ZL = 4, 4, 8, 2, 2
ZH = NZ // ZL
PLANE = NY * NX * NC
HALF = 8
LANES = 128
PIECES = 4
PITCH = 136


def position():
    inp = lax.axis_index("inp")
    tm = lax.axis_index("tm")
    return tm % NX, inp // (ZH * NC), (inp // NC) % ZH * ZL + tm // NX, inp % NC


def device(x, y, z, c):
    return (y * ZH + z // ZL) * NC + c, (z % ZL) * NX + x


def channel_of_row():
    order = np.empty((NY, NX, NC, NZ), np.int64)
    for y in range(NY):
        for x in range(NX):
            for c in range(NC):
                for z in range(NZ):
                    inp, tm = device(x, y, z, c)
                    order[y, x, c, z] = inp * (ZL * NX) + tm
    return order.reshape(-1)


def dft_rows(width):
    channel = channel_of_row()
    phase = (channel[:, None] * np.arange(width)[None, :]) % width
    angle = phase.astype(np.float32) * np.float32(2.0 * math.pi / width)
    rows = np.concatenate([np.cos(angle), -np.sin(angle)], axis=0)
    return rows.astype(ml_dtypes.bfloat16)


def exchange_kernel(
    v_hbm, taps_hbm, table_hbm, r_ref,
    v, taps_ref, table_ref, hist, f32s, s32, sa, sb, za, yb,
    load_sem, hist_send, hist_recv, local_sem,
    za_send, za_recv, xa_send, xa_recv, xb_send, xb_recv, zb_send, zb_recv,
):
    x, y, z, c = position()
    zh, zl = z // ZL, z % ZL
    tm = lax.axis_index("tm")
    inp = lax.axis_index("inp")
    tms = ZL * NX
    taps_n, width = taps_ref.shape
    spectra = v.shape[1] // width
    rows = v.shape[0]
    piece = spectra // PIECES

    def load(g):
        at = pl.ds(pl.multiple_of(g * piece * width, width), piece * width)
        return pltpu.make_async_copy(v_hbm.at[:, at], v.at[:, at], load_sem.at[g])

    load_taps = pltpu.make_async_copy(taps_hbm, taps_ref, load_sem.at[PIECES])
    load_table = pltpu.make_async_copy(table_hbm, table_ref, load_sem.at[PIECES + 1])
    load_taps.start()
    for g in range(PIECES):
        load(g).start()
    load_table.start()

    def z_peer(dz):
        zz = (z + dz) % NZ
        return zz, device(x, y, zz, c)

    def plane_peer(i):
        xx = (x + i // (NY * NC)) % NX
        yy = (y + (i // NC) % NY) % NY
        cc = (c + i % NC) % NC
        return xx, yy, cc, device(xx, yy, z, cc)

    later = (inp, (tm + 1) % tms)
    earlier = (inp, (tm + tms - 1) % tms)
    barrier = pltpu.get_barrier_semaphore()
    pl.semaphore_signal(barrier, inc=1, device_id=later, device_id_type=MESH)
    pl.semaphore_signal(barrier, inc=1, device_id=earlier, device_id_type=MESH)
    for dz in range(1, NZ):
        pl.semaphore_signal(barrier, inc=1, device_id=z_peer(dz)[1], device_id_type=MESH)

    def greet(i, _):
        pl.semaphore_signal(barrier, inc=1, device_id=plane_peer(i)[3], device_id_type=MESH)
        return 0

    lax.fori_loop(1, PLANE, greet, 0)
    pl.semaphore_wait(barrier, 2 + NZ - 1 + PLANE - 1)

    history = pltpu.make_async_remote_copy(
        src_ref=v_hbm.at[:, pl.ds((spectra - (taps_n - 1)) * width, (taps_n - 1) * width)],
        dst_ref=hist,
        send_sem=hist_send,
        recv_sem=hist_recv,
        device_id=later,
        device_id_type=MESH,
    )
    history.start()
    load_taps.wait()

    def block(ref, s, q):
        at = pl.multiple_of(s * width + q * LANES, LANES)
        return ref[:, pl.ds(at, LANES)].astype(jnp.float32)

    def gain(q):
        return [
            jnp.broadcast_to(taps_ref[t : t + 1, q * LANES : (q + 1) * LANES], (rows, LANES))
            for t in range(taps_n)
        ]

    def step(gains, s, q, past):
        past = past + (block(v, s, q),)
        total = gains[0] * past[0]
        for t in range(1, taps_n):
            total = total + gains[t] * past[t]
        f32s.at[q][pl.ds(s, rows, stride=PITCH), :] = total
        return past[1:]

    def filter_piece(g, _):
        load(g).wait()
        for q in range(width // LANES):
            gains = gain(q)
            past = tuple(
                block(v, jnp.maximum(g * piece - k, 0), q) for k in range(taps_n - 1, 0, -1)
            )
            for j in range(piece):
                past = step(gains, g * piece + j, q, past)
        return 0

    lax.fori_loop(0, PIECES, filter_piece, 0)

    history.wait()
    seen = tm > 0
    for q in range(width // LANES):
        gains = gain(q)
        past = tuple(jnp.where(seen, block(hist, s, q), 0.0) for s in range(taps_n - 1))
        for s in range(taps_n - 1):
            past = step(gains, s, q, past)
    load_table.wait()

    def transform(half, out):
        def filtered(i):
            return jnp.concatenate(
                [f32s[q, i * PITCH : i * PITCH + spectra, :] for q in range(width // LANES)],
                axis=1,
            ).astype(jnp.bfloat16)

        for p in range(HALF // 2):
            i = half * HALF + 2 * p
            f = jnp.concatenate([filtered(i), filtered(i + 1)], axis=0)
            spec = lax.dot_general(
                table_ref[...], f, (((1,), (1,)), ((), ())), preferred_element_type=jnp.float32
            )
            for two in range(2):
                for plane in range(2):
                    s32.at[plane][pl.ds(2 * p + two, width // 2, stride=HALF), :] = spec[
                        plane * (width // 2) : (plane + 1) * (width // 2),
                        two * spectra : (two + 1) * spectra,
                    ]

        def pack(m, _):
            at = pl.ds(pl.multiple_of(m * NZ * HALF, NZ * HALF), NZ * HALF)
            both = jnp.concatenate([s32[0, at, :], s32[1, at, :]], axis=1)
            out[m] = both.reshape(NZ, HALF, 2 * spectra).astype(jnp.bfloat16)
            return 0

        lax.fori_loop(0, PLANE, pack, 0)

    here = (y * NX + x) * NC + c

    transform(0, sa)

    def za_copy(dz):
        zz, peer = z_peer(dz)
        return pltpu.make_async_remote_copy(
            src_ref=sa.at[:, zz],
            dst_ref=za.at[zl, zh],
            send_sem=za_send.at[dz - 1],
            recv_sem=za_recv.at[dz - 1],
            device_id=peer,
            device_id_type=MESH,
        )

    for dz in (4, 3, 5, 2, 6, 1, 7):
        za_copy(dz).start()
    keep_a = pltpu.make_async_copy(sa.at[:, z], za.at[zl, zh], local_sem.at[0])
    keep_a.start()

    transform(1, sb)

    def xb_copy(i):
        xx, yy, cc, peer = plane_peer(i)
        return pltpu.make_async_remote_copy(
            src_ref=sb.at[(yy * NX + xx) * NC + cc],
            dst_ref=yb.at[x, y, c],
            send_sem=xb_send.at[i - 1],
            recv_sem=xb_recv.at[i - 1],
            device_id=peer,
            device_id_type=MESH,
        )

    def xb_start(i, _):
        xb_copy(i).start()
        return 0

    lax.fori_loop(1, PLANE, xb_start, 0)
    keep_b = pltpu.make_async_copy(sb.at[here], yb.at[x, y, c], local_sem.at[1])
    keep_b.start()

    def xb_wait(i, _):
        xb_copy(i).wait()
        return 0

    lax.fori_loop(1, PLANE, xb_wait, 0)
    keep_b.wait()

    def zb_copy(dz):
        zz, peer = z_peer(dz)
        return pltpu.make_async_remote_copy(
            src_ref=yb.at[:, :, :, zz],
            dst_ref=r_ref.at[zl, :, :, zh, :, 1],
            send_sem=zb_send.at[dz - 1],
            recv_sem=zb_recv.at[dz - 1],
            device_id=peer,
            device_id_type=MESH,
        )

    for dz in (4, 3, 5, 2, 6, 1, 7):
        zb_copy(dz).start()
    last_b = pltpu.make_async_copy(
        yb.at[:, :, :, z], r_ref.at[zl, :, :, zh, :, 1], local_sem.at[2]
    )
    last_b.start()

    for dz in range(1, NZ):
        za_copy(dz).wait()
    keep_a.wait()

    def xa_copy(i):
        xx, yy, cc, peer = plane_peer(i)
        return pltpu.make_async_remote_copy(
            src_ref=za.at[:, :, (yy * NX + xx) * NC + cc],
            dst_ref=r_ref.at[:, x, y, :, c, 0],
            send_sem=xa_send.at[i - 1],
            recv_sem=xa_recv.at[i - 1],
            device_id=peer,
            device_id_type=MESH,
        )

    def xa_start(i, _):
        xa_copy(i).start()
        return 0

    lax.fori_loop(1, PLANE, xa_start, 0)
    last_a = pltpu.make_async_copy(
        za.at[:, :, here], r_ref.at[:, x, y, :, c, 0], local_sem.at[3]
    )
    last_a.start()

    def xa_wait(i, _):
        xa_copy(i).wait()
        return 0

    lax.fori_loop(1, PLANE, xa_wait, 0)
    last_a.wait()
    for dz in range(1, NZ):
        zb_copy(dz).wait()
    last_b.wait()


def exchange(voltages, taps, table):
    inp_dev, samples = voltages.shape
    width = taps.shape[1]
    spectra = samples // width
    block = (HALF, 2 * spectra)
    bf16 = jnp.bfloat16
    dma = pltpu.SemaphoreType.DMA
    operands = [
        pltpu.with_memory_space_constraint(a, pltpu.HBM) for a in (voltages, taps, table)
    ]
    return pl.pallas_call(
        exchange_kernel,
        name="exchange",
        out_shape=jax.ShapeDtypeStruct((ZL, NX, NY, ZH, NC, inp_dev // HALF) + block, bf16),
        in_specs=[pl.BlockSpec(memory_space=pltpu.HBM)] * 3,
        out_specs=pl.BlockSpec(memory_space=pltpu.VMEM),
        scratch_shapes=[
            pltpu.VMEM((inp_dev, samples), bf16),
            pltpu.VMEM(taps.shape, taps.dtype),
            pltpu.VMEM(table.shape, table.dtype),
            pltpu.VMEM((inp_dev, (taps.shape[0] - 1) * width), bf16),
            pltpu.VMEM((width // LANES, inp_dev * PITCH, LANES), jnp.float32),
            pltpu.VMEM((2, width // 2 * HALF, spectra), jnp.float32),
            pltpu.VMEM((PLANE, NZ) + block, bf16),
            pltpu.VMEM((PLANE, NZ) + block, bf16),
            pltpu.VMEM((ZL, ZH, PLANE) + block, bf16),
            pltpu.VMEM((NX, NY, NC, NZ) + block, bf16),
            dma((PIECES + 2,)), dma(()), dma(()), dma((4,)),
            dma((NZ - 1,)), dma((NZ - 1,)),
            dma((PLANE - 1,)), dma((PLANE - 1,)),
            dma((PLANE - 1,)), dma((PLANE - 1,)),
            dma((NZ - 1,)), dma((NZ - 1,)),
        ],
        compiler_params=pltpu.CompilerParams(
            collective_id=0, has_side_effects=True, vmem_limit_bytes=48 << 20
        ),
    )(*operands)


def correlate_kernel(scale, r_ref, o_hbm, o, sem):
    times, inputs, lanes = r_ref.shape
    half, cut = lanes // 2, inputs // 2

    def product(left, right):
        return scale * lax.dot_general(
            left, right, (((1,), (1,)), ((), ())), preferred_element_type=jnp.float32
        )

    def put(plane, part):
        at = pl.ds(part * cut, cut)
        copy = pltpu.make_async_copy(
            o.at[plane, at], o_hbm.at[0, plane, at], sem.at[2 * plane + part]
        )
        copy.start()
        return copy

    every = jnp.concatenate([r_ref[t] for t in range(times)], axis=1)
    top = product(every[:cut], every)
    o[0, :cut, :] = top
    copies = [put(0, 0)]
    o[0, cut:, cut:] = product(every[cut:], every[cut:])
    o[0, cut:, :cut] = top[:, cut:].T
    copies.append(put(0, 1))
    real = jnp.concatenate([r_ref[t, :, :half] for t in range(times)], axis=1)
    imag = jnp.concatenate([r_ref[t, :, half:] for t in range(times)], axis=1)
    mixed = product(imag, real)
    turned = mixed.T
    o[1, :cut] = mixed[:cut] - turned[:cut]
    copies.append(put(1, 0))
    o[1, cut:] = mixed[cut:] - turned[cut:]
    copies.append(put(1, 1))
    for copy in copies:
        copy.wait()


def correlate(spectra, scale):
    inputs = spectra.shape[1]
    return pl.pallas_call(
        functools.partial(correlate_kernel, scale),
        name="correlate",
        out_shape=jax.ShapeDtypeStruct((1, 2, inputs, inputs), jnp.float32),
        in_specs=[pl.BlockSpec(memory_space=pltpu.VMEM)],
        out_specs=pl.BlockSpec(memory_space=pltpu.HBM),
        scratch_shapes=[
            pltpu.VMEM((2, inputs, inputs), jnp.float32),
            pltpu.SemaphoreType.DMA((4,)),
        ],
        compiler_params=pltpu.CompilerParams(vmem_limit_bytes=32 << 20),
    )(spectra)


def local(voltages, taps):
    width = taps.shape[1]
    table = jnp.asarray(dft_rows(width))
    times = lax.axis_size("tm")
    spectra = voltages.shape[1] // width
    scale = 1.0 / (spectra * times * width)
    gathered = exchange(voltages, taps, table)
    return correlate(gathered.reshape(times, -1, 2 * spectra), scale)


def solution(mesh):
    in_specs = (P("inp", "tm"), P())
    out_specs = P(("inp", "tm"), None, None, None)
    return jax.shard_map(local, mesh=mesh, in_specs=in_specs, out_specs=out_specs, check_vma=False)
```

```python
import functools
import math

import jax
import jax.numpy as jnp
import ml_dtypes
import numpy as np
from jax import lax
from jax.experimental import pallas as pl
from jax.experimental.pallas import tpu as pltpu
from jax.sharding import PartitionSpec as P

MESH = pl.DeviceIdType.MESH
NX, NY, NZ, NC, ZL = 4, 4, 8, 2, 2
ZH = NZ // ZL
PLANE = NY * NX * NC
FAR = NZ // 2
HALF = 8
LANES = 128
PIECES = 4
PITCH = 136


def position():
    inp = lax.axis_index("inp")
    tm = lax.axis_index("tm")
    return tm % NX, inp // (ZH * NC), (inp // NC) % ZH * ZL + tm // NX, inp % NC


def device(x, y, z, c):
    return (y * ZH + z // ZL) * NC + c, (z % ZL) * NX + x


def channel_of_row():
    order = np.empty((NY, NX, NC, NZ), np.int64)
    for y in range(NY):
        for x in range(NX):
            for c in range(NC):
                for z in range(NZ):
                    inp, tm = device(x, y, z, c)
                    order[y, x, c, z] = inp * (ZL * NX) + tm
    return order.reshape(-1)


def dft_rows(width):
    parts = []
    for channel in np.split(channel_of_row(), 2):
        phase = (channel[:, None] * np.arange(width)[None, :]) % width
        angle = phase.astype(np.float32) * np.float32(2.0 * math.pi / width)
        parts += [np.cos(angle), -np.sin(angle)]
    return np.concatenate(parts, axis=0).astype(ml_dtypes.bfloat16)


def exchange_kernel(
    v_hbm, taps_hbm, table_hbm, r_ref,
    v, taps_ref, table_ref, hist, f32s, s32, sa, sb, za, yb, ta, tb,
    load_sem, hist_send, hist_recv, local_sem,
    za_send, za_recv, xa_send, xa_recv, xb_send, xb_recv, zb_send, zb_recv,
):
    x, y, z, c = position()
    zh, zl = z // ZL, z % ZL
    tm = lax.axis_index("tm")
    inp = lax.axis_index("inp")
    tms = ZL * NX
    taps_n, width = taps_ref.shape
    spectra = v.shape[2] // width
    piece = spectra // PIECES
    tail = (taps_n - 1) * width
    group = PLANE // 2

    def load(half, g):
        at = pl.ds(pl.multiple_of(g * piece * width, width), piece * width)
        return pltpu.make_async_copy(
            v_hbm.at[pl.ds(half * HALF, HALF), at], v.at[half, :, at], load_sem.at[half, g]
        )

    load_taps = pltpu.make_async_copy(taps_hbm, taps_ref, load_sem.at[0, PIECES])
    load_table = pltpu.make_async_copy(table_hbm, table_ref, load_sem.at[1, PIECES])
    load_taps.start()
    for half in range(2):
        for g in range(PIECES):
            load(half, g).start()
        if half == 0:
            load_table.start()

    def plane_peer(i):
        xx = (x + i // (NY * NC)) % NX
        yy = (y + (i // NC) % NY) % NY
        cc = (c + i % NC) % NC
        return xx, yy, cc, device(xx, yy, z, cc)

    later = (inp, (tm + 1) % tms)
    earlier = (inp, (tm + tms - 1) % tms)
    beside = (device(x, y, (z + 1) % NZ, c), device(x, y, (z + NZ - 1) % NZ, c))
    barrier = pltpu.get_barrier_semaphore()
    for peer in (earlier, later) + beside:
        pl.semaphore_signal(barrier, inc=1, device_id=peer, device_id_type=MESH)

    def greet(i, _):
        pl.semaphore_signal(barrier, inc=1, device_id=plane_peer(i)[3], device_id_type=MESH)
        return 0

    lax.fori_loop(1, PLANE, greet, 0)
    pl.semaphore_wait(barrier, 4 + PLANE - 1)

    def history(half):
        return pltpu.make_async_remote_copy(
            src_ref=v_hbm.at[pl.ds(half * HALF, HALF), pl.ds(spectra * width - tail, tail)],
            dst_ref=hist.at[half],
            send_sem=hist_send.at[half],
            recv_sem=hist_recv.at[half],
            device_id=later,
            device_id_type=MESH,
        )

    history(0).start()
    history(1).start()
    load_taps.wait()

    def block(ref, half, s, q):
        at = pl.multiple_of(s * width + q * LANES, LANES)
        return ref[half, :, pl.ds(at, LANES)].astype(jnp.float32)

    def gain(q):
        return [
            jnp.broadcast_to(taps_ref[t : t + 1, q * LANES : (q + 1) * LANES], (HALF, LANES))
            for t in range(taps_n)
        ]

    def step(gains, half, s, q, past):
        past = past + (block(v, half, s, q),)
        total = gains[0] * past[0]
        for t in range(1, taps_n):
            total = total + gains[t] * past[t]
        f32s.at[q][pl.ds(half * HALF * PITCH + s, HALF, stride=PITCH), :] = total
        return past[1:]

    def filter_half(half):
        def filter_piece(g, _):
            load(half, g).wait()
            for q in range(width // LANES):
                gains = gain(q)
                past = tuple(
                    block(v, half, jnp.maximum(g * piece - k, 0), q)
                    for k in range(taps_n - 1, 0, -1)
                )
                for j in range(piece):
                    past = step(gains, half, g * piece + j, q, past)
            return 0

        lax.fori_loop(0, PIECES, filter_piece, 0)

    def first_spectra(half):
        history(half).wait()
        for q in range(width // LANES):
            gains = gain(q)
            past = tuple(
                jnp.where(tm > 0, block(hist, half, s, q), 0.0) for s in range(taps_n - 1)
            )
            for s in range(taps_n - 1):
                past = step(gains, half, s, q, past)

    def transform(half, part, out):
        def filtered(i):
            at = (half * HALF + i) * PITCH
            return jnp.concatenate(
                [f32s[q, at : at + spectra, :] for q in range(width // LANES)], axis=1
            ).astype(jnp.bfloat16)

        count = group * NZ
        for i in range(0, HALF, 2):
            f = jnp.concatenate([filtered(i), filtered(i + 1)], axis=0)
            spec = lax.dot_general(
                table_ref[part * 2 * count : (part + 1) * 2 * count, :],
                f,
                (((1,), (1,)), ((), ())),
                preferred_element_type=jnp.float32,
            )
            for two in range(2):
                for plane in range(2):
                    at = pl.ds(part * count * HALF + i + two, count, stride=HALF)
                    s32.at[plane][at, :] = spec[
                        plane * count : (plane + 1) * count,
                        two * spectra : (two + 1) * spectra,
                    ]

        def pack(m, _):
            at = pl.ds(pl.multiple_of(m * NZ * HALF, NZ * HALF), NZ * HALF)
            both = jnp.concatenate([s32[0, at, :], s32[1, at, :]], axis=1)
            out[m] = both.reshape(NZ, HALF, 2 * spectra).astype(jnp.bfloat16)
            return 0

        lax.fori_loop(part * group, (part + 1) * group, pack, 0)

    here = (y * NX + x) * NC + c

    def route(s, d, hop):
        sign = 1 - 2 * s
        source = (z + NZ - (hop - 1) * sign) % NZ
        return source, (source + NZ + d * sign) % NZ

    def za_copy(s, d, hop, part):
        source, target = route(s, d, hop)
        at = pl.ds(part * group, group)
        src = sa.at[at, target] if hop == 1 else ta.at[s, hop - 2, d - 2, at]
        dst = za.at[source % ZL, source // ZL, at] if hop == d else ta.at[s, hop - 1, d - 2, at]
        return pltpu.make_async_remote_copy(
            src_ref=src,
            dst_ref=dst,
            send_sem=za_send.at[s, hop - 1, d - 1, part],
            recv_sem=za_recv.at[s, hop - 1, d - 1, part],
            device_id=beside[s],
            device_id_type=MESH,
        )

    def zb_copy(s, d, hop):
        source, target = route(s, d, hop)
        at = pl.ds(s * (NX // 2), NX // 2) if d == FAR else pl.ds(0, NX)
        src = yb.at[at, :, :, target] if hop == 1 else tb.at[s, hop - 2, d - 2, at]
        dst = (
            r_ref.at[source % ZL, at, :, source // ZL, :, 1]
            if hop == d
            else tb.at[s, hop - 1, d - 2, at]
        )
        return pltpu.make_async_remote_copy(
            src_ref=src,
            dst_ref=dst,
            send_sem=zb_send.at[s, hop - 1, d - 1],
            recv_sem=zb_recv.at[s, hop - 1, d - 1],
            device_id=beside[s],
            device_id_type=MESH,
        )

    def legs_a(d):
        return [(s, part) for part in range(2) for s in range(2) if d < FAR or s == part]

    filter_half(0)
    filter_half(1)
    first_spectra(0)
    load_table.wait()

    for part in range(2):
        transform(0, part, sa)
        for d in range(FAR, 0, -1):
            for s, p in legs_a(d):
                if p == part:
                    za_copy(s, d, 1, p).start()
    keep_a = pltpu.make_async_copy(sa.at[:, z], za.at[zl, zh], local_sem.at[0])
    keep_a.start()

    first_spectra(1)
    for part in range(2):
        transform(1, part, sb)

    def xb_copy(i):
        xx, yy, cc, peer = plane_peer(i)
        return pltpu.make_async_remote_copy(
            src_ref=sb.at[(yy * NX + xx) * NC + cc],
            dst_ref=yb.at[x, y, c],
            send_sem=xb_send.at[i - 1],
            recv_sem=xb_recv.at[i - 1],
            device_id=peer,
            device_id_type=MESH,
        )

    def xb_start(i, _):
        xb_copy(i).start()
        return 0

    lax.fori_loop(1, PLANE, xb_start, 0)
    keep_b = pltpu.make_async_copy(sb.at[here], yb.at[x, y, c], local_sem.at[1])
    keep_b.start()

    for hop in range(2, FAR + 1):
        for d in range(FAR, hop - 1, -1):
            for s, p in legs_a(d):
                za_copy(s, d, hop - 1, p).wait_recv()
                za_copy(s, d, hop, p).start()

    def xb_wait(i, _):
        xb_copy(i).wait()
        return 0

    lax.fori_loop(1, PLANE, xb_wait, 0)
    keep_b.wait()

    for d in range(FAR, 0, -1):
        for s in range(2):
            zb_copy(s, d, 1).start()
    last_b = pltpu.make_async_copy(
        yb.at[:, :, :, z], r_ref.at[zl, :, :, zh, :, 1], local_sem.at[2]
    )
    last_b.start()

    for d in range(1, FAR + 1):
        for s, p in legs_a(d):
            za_copy(s, d, d, p).wait_recv()
    keep_a.wait()

    def xa_copy(i):
        xx, yy, cc, peer = plane_peer(i)
        return pltpu.make_async_remote_copy(
            src_ref=za.at[:, :, (yy * NX + xx) * NC + cc],
            dst_ref=r_ref.at[:, x, y, :, c, 0],
            send_sem=xa_send.at[i - 1],
            recv_sem=xa_recv.at[i - 1],
            device_id=peer,
            device_id_type=MESH,
        )

    def xa_start(i, _):
        xa_copy(i).start()
        return 0

    lax.fori_loop(1, PLANE, xa_start, 0)
    last_a = pltpu.make_async_copy(
        za.at[:, :, here], r_ref.at[:, x, y, :, c, 0], local_sem.at[3]
    )
    last_a.start()

    for hop in range(2, FAR + 1):
        for d in range(FAR, hop - 1, -1):
            for s in range(2):
                zb_copy(s, d, hop - 1).wait_recv()
                zb_copy(s, d, hop).start()

    for d in range(1, FAR + 1):
        for hop in range(1, d + 1):
            for s, p in legs_a(d):
                za_copy(s, d, hop, p).wait_send()

    def xa_wait(i, _):
        xa_copy(i).wait()
        return 0

    lax.fori_loop(1, PLANE, xa_wait, 0)
    last_a.wait()
    last_b.wait()
    for d in range(1, FAR + 1):
        for s in range(2):
            zb_copy(s, d, d).wait_recv()
    for d in range(1, FAR + 1):
        for hop in range(1, d + 1):
            for s in range(2):
                zb_copy(s, d, hop).wait_send()


def exchange(voltages, taps, table):
    inp_dev, samples = voltages.shape
    width = taps.shape[1]
    spectra = samples // width
    block = (HALF, 2 * spectra)
    bf16 = jnp.bfloat16
    dma = pltpu.SemaphoreType.DMA
    operands = [
        pltpu.with_memory_space_constraint(a, pltpu.HBM) for a in (voltages, taps, table)
    ]
    return pl.pallas_call(
        exchange_kernel,
        name="exchange",
        out_shape=jax.ShapeDtypeStruct((ZL, NX, NY, ZH, NC, inp_dev // HALF) + block, bf16),
        in_specs=[pl.BlockSpec(memory_space=pltpu.HBM)] * 3,
        out_specs=pl.BlockSpec(memory_space=pltpu.VMEM),
        scratch_shapes=[
            pltpu.VMEM((2, HALF, samples), bf16),
            pltpu.VMEM(taps.shape, taps.dtype),
            pltpu.VMEM(table.shape, table.dtype),
            pltpu.VMEM((2, HALF, (taps.shape[0] - 1) * width), bf16),
            pltpu.VMEM((width // LANES, inp_dev * PITCH, LANES), jnp.float32),
            pltpu.VMEM((2, width // 2 * HALF, spectra), jnp.float32),
            pltpu.VMEM((PLANE, NZ) + block, bf16),
            pltpu.VMEM((PLANE, NZ) + block, bf16),
            pltpu.VMEM((ZL, ZH, PLANE) + block, bf16),
            pltpu.VMEM((NX, NY, NC, NZ) + block, bf16),
            pltpu.VMEM((2, FAR - 1, FAR - 1, PLANE) + block, bf16),
            pltpu.VMEM((2, FAR - 1, FAR - 1, NX, NY, NC) + block, bf16),
            dma((2, PIECES + 1)), dma((2,)), dma((2,)), dma((4,)),
            dma((2, FAR, FAR, 2)), dma((2, FAR, FAR, 2)),
            dma((PLANE - 1,)), dma((PLANE - 1,)),
            dma((PLANE - 1,)), dma((PLANE - 1,)),
            dma((2, FAR, FAR)), dma((2, FAR, FAR)),
        ],
        compiler_params=pltpu.CompilerParams(
            collective_id=0, has_side_effects=True, vmem_limit_bytes=48 << 20
        ),
    )(*operands)


def correlate_kernel(scale, r_ref, o_hbm, o, sem):
    times, inputs, lanes = r_ref.shape
    half, cut = lanes // 2, inputs // 2

    def product(left, right):
        return scale * lax.dot_general(
            left, right, (((1,), (1,)), ((), ())), preferred_element_type=jnp.float32
        )

    def put(plane, part):
        at = pl.ds(part * cut, cut)
        copy = pltpu.make_async_copy(
            o.at[plane, at], o_hbm.at[0, plane, at], sem.at[2 * plane + part]
        )
        copy.start()
        return copy

    every = jnp.concatenate([r_ref[t] for t in range(times)], axis=1)
    top = product(every[:cut], every)
    o[0, :cut, :] = top
    copies = [put(0, 0)]
    o[0, cut:, cut:] = product(every[cut:], every[cut:])
    o[0, cut:, :cut] = top[:, cut:].T
    copies.append(put(0, 1))
    real = jnp.concatenate([r_ref[t, :, :half] for t in range(times)], axis=1)
    imag = jnp.concatenate([r_ref[t, :, half:] for t in range(times)], axis=1)
    mixed = product(imag, real)
    turned = mixed.T
    o[1, :cut] = mixed[:cut] - turned[:cut]
    copies.append(put(1, 0))
    o[1, cut:] = mixed[cut:] - turned[cut:]
    copies.append(put(1, 1))
    for copy in copies:
        copy.wait()


def correlate(spectra, scale):
    inputs = spectra.shape[1]
    return pl.pallas_call(
        functools.partial(correlate_kernel, scale),
        name="correlate",
        out_shape=jax.ShapeDtypeStruct((1, 2, inputs, inputs), jnp.float32),
        in_specs=[pl.BlockSpec(memory_space=pltpu.VMEM)],
        out_specs=pl.BlockSpec(memory_space=pltpu.HBM),
        scratch_shapes=[
            pltpu.VMEM((2, inputs, inputs), jnp.float32),
            pltpu.SemaphoreType.DMA((4,)),
        ],
        compiler_params=pltpu.CompilerParams(vmem_limit_bytes=32 << 20),
    )(spectra)


def local(voltages, taps):
    width = taps.shape[1]
    table = jnp.asarray(dft_rows(width))
    times = lax.axis_size("tm")
    spectra = voltages.shape[1] // width
    scale = 1.0 / (spectra * times * width)
    gathered = exchange(voltages, taps, table)
    return correlate(gathered.reshape(times, -1, 2 * spectra), scale)


def solution(mesh):
    in_specs = (P("inp", "tm"), P())
    out_specs = P(("inp", "tm"), None, None, None)
    return jax.shard_map(local, mesh=mesh, in_specs=in_specs, out_specs=out_specs, check_vma=False)
```

```python
import functools
import math

import jax
import jax.numpy as jnp
import ml_dtypes
import numpy as np
from jax import lax
from jax.experimental import pallas as pl
from jax.experimental.pallas import tpu as pltpu
from jax.sharding import PartitionSpec as P

MESH = pl.DeviceIdType.MESH
NX, NY, NZ, NC, ZL = 4, 4, 8, 2, 2
ZH = NZ // ZL
PLANE = NY * NX * NC
FAR = NZ // 2
HALF = 8
LANES = 128
PIECES = 4
PITCH = 136


def position():
    inp = lax.axis_index("inp")
    tm = lax.axis_index("tm")
    return tm % NX, inp // (ZH * NC), (inp // NC) % ZH * ZL + tm // NX, inp % NC


def device(x, y, z, c):
    return (y * ZH + z // ZL) * NC + c, (z % ZL) * NX + x


def channel_of_row():
    order = np.empty((NC, NZ, NY, NX), np.int64)
    for c in range(NC):
        for z in range(NZ):
            for y in range(NY):
                for x in range(NX):
                    inp, tm = device(x, y, z, c)
                    order[c, z, y, x] = inp * (ZL * NX) + tm
    return order.reshape(-1)


def dft_rows(width):
    parts = []
    for channel in np.split(channel_of_row(), NC):
        phase = (channel[:, None] * np.arange(width)[None, :]) % width
        angle = phase.astype(np.float32) * np.float32(2.0 * math.pi / width)
        parts += [np.cos(angle), -np.sin(angle)]
    return np.concatenate(parts, axis=0).astype(ml_dtypes.bfloat16)


def exchange_kernel(
    v_hbm, taps_hbm, table_hbm, r_ref,
    v, taps_ref, table_ref, hist, f32s, s32, sa, sb, za, yb, ta, tb, ca, cb, xa, xb, via0, via1,
    load_sem, hist_send, hist_recv, local_sem,
    ready, core_send, core_recv, za_send, za_recv, zb_send, zb_recv, plane_send, plane_recv,
):
    x, y, z, c = position()
    zh, zl = z // ZL, z % ZL
    tm = lax.axis_index("tm")
    inp = lax.axis_index("inp")
    tms = ZL * NX
    taps_n, width = taps_ref.shape
    spectra = v.shape[2] // width
    piece = spectra // PIECES
    tail = (taps_n - 1) * width
    count = NZ * NY * NX

    def load(half, g):
        at = pl.ds(pl.multiple_of(g * piece * width, width), piece * width)
        return pltpu.make_async_copy(
            v_hbm.at[pl.ds(half * HALF, HALF), at], v.at[half, :, at], load_sem.at[half, g]
        )

    load_taps = pltpu.make_async_copy(taps_hbm, taps_ref, load_sem.at[0, PIECES])
    load_table = pltpu.make_async_copy(table_hbm, table_ref, load_sem.at[1, PIECES])
    load_taps.start()
    for half in range(2):
        for g in range(PIECES):
            load(half, g).start()
        if half == 0:
            load_table.start()

    beside = (
        (device(x, y, (z + 1) % NZ, c), device(x, y, (z + NZ - 1) % NZ, c)),
        (device((x + 1) % NX, y, z, c), device((x + NX - 1) % NX, y, z, c)),
        (device(x, (y + 1) % NY, z, c), device(x, (y + NY - 1) % NY, z, c)),
    )
    twin = device(x, y, z, 1 - c)
    later = (inp, (tm + 1) % tms)
    earlier = (inp, (tm + tms - 1) % tms)

    barrier = pltpu.get_barrier_semaphore()
    callers = (beside[0][1], beside[1][1], beside[2][1], twin, earlier)
    for peer in callers:
        pl.semaphore_signal(barrier, inc=1, device_id=peer, device_id_type=MESH)
    pl.semaphore_wait(barrier, len(callers))
    for axis in range(3):
        pl.semaphore_signal(
            ready.at[axis], inc=1, device_id=beside[axis][0], device_id_type=MESH
        )

    def history(half):
        return pltpu.make_async_remote_copy(
            src_ref=v_hbm.at[pl.ds(half * HALF, HALF), pl.ds(spectra * width - tail, tail)],
            dst_ref=hist.at[half],
            send_sem=hist_send.at[half],
            recv_sem=hist_recv.at[half],
            device_id=later,
            device_id_type=MESH,
        )

    history(0).start()
    history(1).start()
    load_taps.wait()

    def block(ref, half, s, q):
        at = pl.multiple_of(s * width + q * LANES, LANES)
        return ref[half, :, pl.ds(at, LANES)].astype(jnp.float32)

    def gain(q):
        return [
            jnp.broadcast_to(taps_ref[t : t + 1, q * LANES : (q + 1) * LANES], (HALF, LANES))
            for t in range(taps_n)
        ]

    def step(gains, half, s, q, past):
        past = past + (block(v, half, s, q),)
        total = gains[0] * past[0]
        for t in range(1, taps_n):
            total = total + gains[t] * past[t]
        f32s.at[q][pl.ds(half * HALF * PITCH + s, HALF, stride=PITCH), :] = total
        return past[1:]

    def filter_half(half):
        def filter_piece(g, _):
            load(half, g).wait()
            for q in range(width // LANES):
                gains = gain(q)
                past = tuple(
                    block(v, half, jnp.maximum(g * piece - k, 0), q)
                    for k in range(taps_n - 1, 0, -1)
                )
                for j in range(piece):
                    past = step(gains, half, g * piece + j, q, past)
            return 0

        lax.fori_loop(0, PIECES, filter_piece, 0)

    def first_spectra(half):
        history(half).wait()
        for q in range(width // LANES):
            gains = gain(q)
            past = tuple(
                jnp.where(tm > 0, block(hist, half, s, q), 0.0) for s in range(taps_n - 1)
            )
            for s in range(taps_n - 1):
                past = step(gains, half, s, q, past)

    def transform(half, part, out):
        def filtered(i):
            at = (half * HALF + i) * PITCH
            return jnp.concatenate(
                [f32s[q, at : at + spectra, :] for q in range(width // LANES)], axis=1
            ).astype(jnp.bfloat16)

        for i in range(0, HALF, 2):
            f = jnp.concatenate([filtered(i), filtered(i + 1)], axis=0)
            spec = lax.dot_general(
                table_ref[part * 2 * count : (part + 1) * 2 * count, :],
                f,
                (((1,), (1,)), ((), ())),
                preferred_element_type=jnp.float32,
            )
            for two in range(2):
                for plane in range(2):
                    at = pl.ds(part * count * HALF + i + two, count, stride=HALF)
                    s32.at[plane][at, :] = spec[
                        plane * count : (plane + 1) * count,
                        two * spectra : (two + 1) * spectra,
                    ]

        def pack(m, _):
            size = NY * NX * HALF
            at = pl.ds(pl.multiple_of((part * NZ + m) * size, size), size)
            both = jnp.concatenate([s32[0, at, :], s32[1, at, :]], axis=1)
            out[part, m] = both.reshape(NY, NX, HALF, 2 * spectra).astype(jnp.bfloat16)
            return 0

        lax.fori_loop(0, NZ, pack, 0)

    def route(s, d, hop):
        sign = 1 - 2 * s
        source = (z + NZ - (hop - 1) * sign) % NZ
        return source, (source + NZ + d * sign) % NZ

    def remote(src, dst, send, recv, peer):
        return pltpu.make_async_remote_copy(
            src_ref=src,
            dst_ref=dst,
            send_sem=send,
            recv_sem=recv,
            device_id=peer,
            device_id_type=MESH,
        )

    def za_copy(s, d, hop, part):
        source, target = route(s, d, hop)
        src = sa.at[part, target] if hop == 1 else ta.at[s, hop - 2, d - 2, part]
        dst = (
            za.at[part, source % ZL * ZH + source // ZL]
            if hop == d
            else ta.at[s, hop - 1, d - 2, part]
        )
        at = (s, hop - 1, d - 1, part)
        return remote(src, dst, za_send.at[at], za_recv.at[at], beside[0][s])

    def zb_copy(s, d, hop):
        source, target = route(s, d, hop)
        at = pl.ds(s * (NX // 2), NX // 2) if d == FAR else pl.ds(0, NX)
        src = yb.at[at, :, target] if hop == 1 else tb.at[s, hop - 2, d - 2, at]
        dst = (
            r_ref.at[source % ZL, at, :, source // ZL, :, 1]
            if hop == d
            else tb.at[s, hop - 1, d - 2, at]
        )
        at = (s, hop - 1, d - 1)
        return remote(src, dst, zb_send.at[at], zb_recv.at[at], beside[0][s])

    stage, rings, passing = (ca, cb), (xa, xb), (via0, via1)
    per = NZ // 2

    def core_copy(half, src):
        return remote(
            src.at[1 - c], stage[half].at[:, c], core_send.at[half], core_recv.at[half], twin
        )

    def own_core(half, src):
        return pltpu.make_async_copy(
            src.at[c], stage[half].at[:, c], local_sem.at[half, 0]
        )

    def leg_src(half, unit, leg, to, lo, n):
        along_x = unit == leg
        if leg == 1:
            return rings[half].at[unit, :, pl.ds(lo, n), :, to]
        at = pl.ds(unit * per + lo, n)
        return stage[half].at[at, :, :, to] if along_x else stage[half].at[at, :, to]

    def leg_dst(half, unit, leg, frm, lo, n):
        along_x = unit == leg
        if leg == 0:
            return rings[half].at[unit, frm, pl.ds(lo, n)]
        if half == 0:
            at = pl.ds(lo, n)
            if along_x:
                return r_ref.at[unit, frm, :, at, :, 0]
            return r_ref.at[unit, :, frm, at, :, 0]
        at = pl.ds(unit * per + lo, n)
        return yb.at[frm, :, at] if along_x else yb.at[:, frm, at]

    def plane_copy(half, unit, leg, s, kind):
        along_x = unit == leg
        size, mine = (NX, x) if along_x else (NY, y)
        sign = 1 - 2 * s
        lo, n = (0, per) if kind == 0 else (s * per // 2, per // 2)
        peer = beside[1 if along_x else 2][s]
        via = passing[leg].at[half, unit, s]
        if kind == 0:
            src = leg_src(half, unit, leg, (mine + size + sign) % size, lo, n)
            dst = leg_dst(half, unit, leg, mine, lo, n)
        elif kind == 1:
            src = leg_src(half, unit, leg, (mine + 2) % size, lo, n)
            dst = via
        else:
            src = via
            dst = leg_dst(half, unit, leg, (mine + size - sign) % size, lo, n)
        at = (half, unit, leg, s, kind)
        return remote(src, dst, plane_send.at[at], plane_recv.at[at], peer)

    def own_leg(half, unit, leg):
        mine = x if unit == leg else y
        return pltpu.make_async_copy(
            leg_src(half, unit, leg, mine, 0, per),
            leg_dst(half, unit, leg, mine, 0, per),
            local_sem.at[half, 1 + 2 * unit + leg],
        )

    every_leg = [(unit, s) for unit in range(2) for s in range(2)]

    def legs_start(half, leg, first=False):
        for s in range(2):
            if first and s == 1:
                pl.semaphore_wait(ready.at[1], 1)
                pl.semaphore_wait(ready.at[2], 1)
            for kind in (1, 0):
                for unit in range(2):
                    plane_copy(half, unit, leg, s, kind).start()
        for unit in range(2):
            own_leg(half, unit, leg).start()

    def legs_forward(half, leg):
        for unit, s in every_leg:
            plane_copy(half, unit, leg, s, 1).wait_recv()
            plane_copy(half, unit, leg, s, 2).start()

    def legs_wait(half, leg):
        for unit, s in every_leg:
            plane_copy(half, unit, leg, s, 0).wait_recv()
            plane_copy(half, unit, leg, s, 2).wait_recv()
        for unit in range(2):
            own_leg(half, unit, leg).wait()

    def za_forward(hop):
        for d in range(FAR, hop - 1, -1):
            for s, p in legs_a(d):
                za_copy(s, d, hop - 1, p).wait_recv()
                za_copy(s, d, hop, p).start()

    def zb_forward(hop):
        for d in range(FAR, hop - 1, -1):
            for s in range(2):
                zb_copy(s, d, hop - 1).wait_recv()
                zb_copy(s, d, hop).start()

    def legs_a(d):
        return [(s, part) for part in range(2) for s in range(2) if d < FAR or s == part]

    filter_half(0)
    filter_half(1)
    first_spectra(0)
    load_table.wait()

    for part in range(NC):
        transform(0, part, sa)
        for s in range(2):
            if part == 0 and s == 1:
                pl.semaphore_wait(ready.at[0], 1)
            for d in range(FAR, 0, -1):
                if (s, part) in legs_a(d):
                    za_copy(s, d, 1, part).start()
    keep_a = pltpu.make_async_copy(sa.at[:, z], za.at[:, zl * ZH + zh], local_sem.at[0, 5])
    keep_a.start()

    first_spectra(1)
    for part in range(NC):
        transform(1, part, sb)
    core_copy(1, sb).start()
    own_core(1, sb).start()
    core_copy(1, sb).wait()
    own_core(1, sb).wait()
    legs_start(1, 0, first=True)
    za_forward(2)
    legs_forward(1, 0)
    legs_wait(1, 0)
    legs_start(1, 1)
    za_forward(3)
    legs_forward(1, 1)
    za_forward(4)
    legs_wait(1, 1)

    for d in range(FAR, 0, -1):
        for s in range(2):
            zb_copy(s, d, 1).start()
    last_b = pltpu.make_async_copy(
        yb.at[:, :, z], r_ref.at[zl, :, :, zh, :, 1], local_sem.at[1, 5]
    )
    last_b.start()

    for d in range(1, FAR + 1):
        for s, p in legs_a(d):
            za_copy(s, d, d, p).wait_recv()
    keep_a.wait()
    core_copy(0, za).start()
    own_core(0, za).start()
    core_copy(0, za).wait()
    own_core(0, za).wait()
    legs_start(0, 0)
    zb_forward(2)
    legs_forward(0, 0)
    legs_wait(0, 0)
    legs_start(0, 1)
    zb_forward(3)
    legs_forward(0, 1)
    zb_forward(4)

    for d in range(1, FAR + 1):
        for hop in range(1, d + 1):
            for s, p in legs_a(d):
                za_copy(s, d, hop, p).wait_send()
    for half in (1, 0):
        for leg in range(2):
            for unit, s in every_leg:
                for kind in range(3):
                    plane_copy(half, unit, leg, s, kind).wait_send()
    legs_wait(0, 1)
    last_b.wait()
    for d in range(1, FAR + 1):
        for s in range(2):
            zb_copy(s, d, d).wait_recv()
    for d in range(1, FAR + 1):
        for hop in range(1, d + 1):
            for s in range(2):
                zb_copy(s, d, hop).wait_send()


def exchange(voltages, taps, table):
    inp_dev, samples = voltages.shape
    width = taps.shape[1]
    spectra = samples // width
    block = (HALF, 2 * spectra)
    bf16 = jnp.bfloat16
    dma = pltpu.SemaphoreType.DMA
    operands = [
        pltpu.with_memory_space_constraint(a, pltpu.HBM) for a in (voltages, taps, table)
    ]
    return pl.pallas_call(
        exchange_kernel,
        name="exchange",
        out_shape=jax.ShapeDtypeStruct((ZL, NX, NY, ZH, NC, inp_dev // HALF) + block, bf16),
        in_specs=[pl.BlockSpec(memory_space=pltpu.HBM)] * 3,
        out_specs=pl.BlockSpec(memory_space=pltpu.VMEM),
        scratch_shapes=[
            pltpu.VMEM((2, HALF, samples), bf16),
            pltpu.VMEM(taps.shape, taps.dtype),
            pltpu.VMEM(table.shape, table.dtype),
            pltpu.VMEM((2, HALF, (taps.shape[0] - 1) * width), bf16),
            pltpu.VMEM((width // LANES, inp_dev * PITCH, LANES), jnp.float32),
            pltpu.VMEM((2, width // 2 * HALF, spectra), jnp.float32),
            pltpu.VMEM((NC, NZ, NY, NX) + block, bf16),
            pltpu.VMEM((NC, NZ, NY, NX) + block, bf16),
            pltpu.VMEM((NC, NZ, NY, NX) + block, bf16),
            pltpu.VMEM((NX, NY, NZ, NC) + block, bf16),
            pltpu.VMEM((2, FAR - 1, FAR - 1, NC, NY, NX) + block, bf16),
            pltpu.VMEM((2, FAR - 1, FAR - 1, NX, NY, NC) + block, bf16),
            pltpu.VMEM((NZ, NC, NY, NX) + block, bf16),
            pltpu.VMEM((NZ, NC, NY, NX) + block, bf16),
            pltpu.VMEM((2, NX, NZ // 2, NC, NY) + block, bf16),
            pltpu.VMEM((2, NX, NZ // 2, NC, NY) + block, bf16),
            pltpu.VMEM((2, 2, 2, NZ // 4, NC, NY) + block, bf16),
            pltpu.VMEM((2, 2, 2, NX, NZ // 4, NC) + block, bf16),
            dma((2, PIECES + 1)), dma((2,)), dma((2,)), dma((2, 6)),
            pltpu.SemaphoreType.REGULAR((3,)), dma((2,)), dma((2,)),
            dma((2, FAR, FAR, NC)), dma((2, FAR, FAR, NC)),
            dma((2, FAR, FAR)), dma((2, FAR, FAR)),
            dma((2, 2, 2, 2, 3)), dma((2, 2, 2, 2, 3)),
        ],
        compiler_params=pltpu.CompilerParams(
            collective_id=0, has_side_effects=True, vmem_limit_bytes=48 << 20
        ),
    )(*operands)


def correlate_kernel(scale, r_ref, o_hbm, o, sem):
    times, inputs, lanes = r_ref.shape
    half, cut = lanes // 2, inputs // 2

    def product(left, right):
        return scale * lax.dot_general(
            left, right, (((1,), (1,)), ((), ())), preferred_element_type=jnp.float32
        )

    def put(plane, part):
        at = pl.ds(part * cut, cut)
        copy = pltpu.make_async_copy(
            o.at[plane, at], o_hbm.at[0, plane, at], sem.at[2 * plane + part]
        )
        copy.start()
        return copy

    every = jnp.concatenate([r_ref[t] for t in range(times)], axis=1)
    top = product(every[:cut], every)
    o[0, :cut, :] = top
    copies = [put(0, 0)]
    o[0, cut:, cut:] = product(every[cut:], every[cut:])
    o[0, cut:, :cut] = top[:, cut:].T
    copies.append(put(0, 1))
    real = jnp.concatenate([r_ref[t, :, :half] for t in range(times)], axis=1)
    imag = jnp.concatenate([r_ref[t, :, half:] for t in range(times)], axis=1)
    mixed = product(imag, real)
    turned = mixed.T
    o[1, :cut] = mixed[:cut] - turned[:cut]
    copies.append(put(1, 0))
    o[1, cut:] = mixed[cut:] - turned[cut:]
    copies.append(put(1, 1))
    for copy in copies:
        copy.wait()


def correlate(spectra, scale):
    inputs = spectra.shape[1]
    return pl.pallas_call(
        functools.partial(correlate_kernel, scale),
        name="correlate",
        out_shape=jax.ShapeDtypeStruct((1, 2, inputs, inputs), jnp.float32),
        in_specs=[pl.BlockSpec(memory_space=pltpu.VMEM)],
        out_specs=pl.BlockSpec(memory_space=pltpu.HBM),
        scratch_shapes=[
            pltpu.VMEM((2, inputs, inputs), jnp.float32),
            pltpu.SemaphoreType.DMA((4,)),
        ],
        compiler_params=pltpu.CompilerParams(vmem_limit_bytes=32 << 20),
    )(spectra)


def local(voltages, taps):
    width = taps.shape[1]
    table = jnp.asarray(dft_rows(width))
    times = lax.axis_size("tm")
    spectra = voltages.shape[1] // width
    scale = 1.0 / (spectra * times * width)
    gathered = exchange(voltages, taps, table)
    return correlate(gathered.reshape(times, -1, 2 * spectra), scale)


def solution(mesh):
    in_specs = (P("inp", "tm"), P())
    out_specs = P(("inp", "tm"), None, None, None)
    return jax.shard_map(local, mesh=mesh, in_specs=in_specs, out_specs=out_specs, check_vma=False)
```

```python
import functools
import math

import jax
import jax.numpy as jnp
import ml_dtypes
import numpy as np
from jax import lax
from jax.experimental import pallas as pl
from jax.experimental.pallas import tpu as pltpu
from jax.sharding import PartitionSpec as P

MESH = pl.DeviceIdType.MESH
NX, NY, NZ, NC, ZL = 4, 4, 8, 2, 2
ZH = NZ // ZL
PLANE = NY * NX * NC
FAR = NZ // 2
LANES = 128
PIECES = 8
PITCH = 136


def position():
    inp = lax.axis_index("inp")
    tm = lax.axis_index("tm")
    return tm % NX, inp // (ZH * NC), (inp // NC) % ZH * ZL + tm // NX, inp % NC


def device(x, y, z, c):
    return (y * ZH + z // ZL) * NC + c, (z % ZL) * NX + x


def channel_of_row():
    order = np.empty((NC, NZ, NY, NX), np.int64)
    for c in range(NC):
        for z in range(NZ):
            for y in range(NY):
                for x in range(NX):
                    inp, tm = device(x, y, z, c)
                    order[c, z, y, x] = inp * (ZL * NX) + tm
    return order.reshape(-1)


def dft_rows(width):
    parts = []
    for channel in np.split(channel_of_row(), NC):
        phase = (channel[:, None] * np.arange(width)[None, :]) % width
        angle = phase.astype(np.float32) * np.float32(2.0 * math.pi / width)
        parts += [np.cos(angle), -np.sin(angle)]
    return np.concatenate(parts, axis=0).astype(ml_dtypes.bfloat16)


def products(ref):
    inputs = NY * ZH * NC * ref.shape[5]
    cut = inputs // 2
    times = [ref[t // NX, t % NX].reshape(inputs, LANES) for t in range(ZL * NX)]
    every = jnp.concatenate(times, axis=1)
    half = LANES // 2
    turned = jnp.concatenate(
        [part for t in times for part in (t[:, half:], -t[:, :half])], axis=1
    )
    for plane, left in ((0, every), (1, turned)):
        for low in (False, True):
            at = slice(cut, inputs) if low else slice(0, cut)
            yield plane, low, lax.dot_general(
                left[at],
                every[cut:] if low else every,
                (((1,), (1,)), ((), ())),
                preferred_element_type=jnp.float32,
            )


def exchange_kernel(
    v_hbm, taps_hbm, table_hbm, rb, sums, ra,
    v, taps_ref, table_ref, hist, f32s, s32, sa, sb, za, yb, ta, tb, ca, cb, xa, xb, via0, via1,
    load_sem, hist_send, hist_recv, local_sem,
    ready, core_send, core_recv, za_send, za_recv, zb_send, zb_recv, plane_send, plane_recv,
):
    x, y, z, c = position()
    zh, zl = z // ZL, z % ZL
    tm = lax.axis_index("tm")
    inp = lax.axis_index("inp")
    tms = ZL * NX
    taps_n, width = taps_ref.shape
    rows = v.shape[0]
    spectra = v.shape[1] // width
    piece = spectra // PIECES
    span = spectra // 2
    tail = (taps_n - 1) * width
    count = NZ * NY * NX
    cut = sums.shape[1] // 2

    def load(g):
        at = pl.ds(pl.multiple_of(g * piece * width, width), piece * width)
        return pltpu.make_async_copy(v_hbm.at[:, at], v.at[:, at], load_sem.at[g])

    load_taps = pltpu.make_async_copy(taps_hbm, taps_ref, load_sem.at[PIECES])
    load_table = pltpu.make_async_copy(table_hbm, table_ref, load_sem.at[PIECES + 1])
    middle = PIECES // 2
    load_taps.start()
    for g in range(middle - 1, PIECES):
        load(g).start()
    load_table.start()
    for g in range(middle - 1):
        load(g).start()

    beside = (
        (device(x, y, (z + 1) % NZ, c), device(x, y, (z + NZ - 1) % NZ, c)),
        (device((x + 1) % NX, y, z, c), device((x + NX - 1) % NX, y, z, c)),
        (device(x, (y + 1) % NY, z, c), device(x, (y + NY - 1) % NY, z, c)),
    )
    twin = device(x, y, z, 1 - c)
    later = (inp, (tm + 1) % tms)
    earlier = (inp, (tm + tms - 1) % tms)

    barrier = pltpu.get_barrier_semaphore()
    callers = (beside[0][1], beside[1][1], beside[2][1], twin, earlier)
    for peer in callers:
        pl.semaphore_signal(barrier, inc=1, device_id=peer, device_id_type=MESH)
    pl.semaphore_wait(barrier, len(callers))
    for axis in range(3):
        pl.semaphore_signal(
            ready.at[axis], inc=1, device_id=beside[axis][0], device_id_type=MESH
        )

    history = pltpu.make_async_remote_copy(
        src_ref=v_hbm.at[:, pl.ds(spectra * width - tail, tail)],
        dst_ref=hist,
        send_sem=hist_send,
        recv_sem=hist_recv,
        device_id=later,
        device_id_type=MESH,
    )
    history.start()
    load_taps.wait()

    def block(ref, s, q):
        at = pl.multiple_of(s * width + q * LANES, LANES)
        return ref[:, pl.ds(at, LANES)].astype(jnp.float32)

    def gain(q):
        return [
            jnp.broadcast_to(taps_ref[t : t + 1, q * LANES : (q + 1) * LANES], (rows, LANES))
            for t in range(taps_n)
        ]

    def step(gains, s, q, past):
        past = past + (block(v, s, q),)
        total = gains[0] * past[0]
        for t in range(1, taps_n):
            total = total + gains[t] * past[t]
        f32s.at[q][pl.ds(s, rows, stride=PITCH), :] = total
        return past[1:]

    def filter_pieces(lo, hi, wait):
        def filter_piece(g, _):
            if wait:
                load(g).wait()
            for q in range(width // LANES):
                gains = gain(q)
                past = tuple(
                    block(v, jnp.maximum(g * piece - k, 0), q) for k in range(taps_n - 1, 0, -1)
                )
                for j in range(piece):
                    past = step(gains, g * piece + j, q, past)
            return 0

        lax.fori_loop(lo, hi, filter_piece, 0)

    def first_spectra():
        history.wait()
        for q in range(width // LANES):
            gains = gain(q)
            past = tuple(jnp.where(tm > 0, block(hist, s, q), 0.0) for s in range(taps_n - 1))
            for s in range(taps_n - 1):
                past = step(gains, s, q, past)

    def transform(half, part, out):
        first = lax.broadcasted_iota(jnp.int32, (count, LANES), 1) < span

        def filtered(i):
            at = i * PITCH + (1 - half) * span
            return jnp.concatenate(
                [f32s[q, at : at + span, :] for q in range(width // LANES)], axis=1
            ).astype(jnp.bfloat16)

        for i in range(0, rows, 4):
            spec = lax.dot_general(
                table_ref[part * 2 * count : (part + 1) * 2 * count, :],
                jnp.concatenate([filtered(i + k) for k in range(4)], axis=0),
                (((1,), (1,)), ((), ())),
                preferred_element_type=jnp.float32,
            )
            for two in range(2):
                real = spec[:count, two * LANES : (two + 1) * LANES]
                imag = spec[count:, two * LANES : (two + 1) * LANES]
                pairs = (
                    jnp.where(first, real, pltpu.roll(imag, span, 1)),
                    jnp.where(first, pltpu.roll(real, span, 1), imag),
                )
                for k in range(2):
                    at = pl.ds(part * count * rows + i + 2 * two + k, count, stride=rows)
                    s32[at, :] = pairs[k]

        def pack(m, _):
            size = NY * NX * rows
            at = pl.ds(pl.multiple_of((part * NZ + m) * size, size), size)
            out[part, m] = s32[at, :].reshape(NY, NX, rows, LANES).astype(jnp.bfloat16)
            return 0

        lax.fori_loop(0, NZ, pack, 0)

    def route(s, d, hop):
        sign = 1 - 2 * s
        source = (z + NZ - (hop - 1) * sign) % NZ
        return source, (source + NZ + d * sign) % NZ

    def remote(src, dst, send, recv, peer):
        return pltpu.make_async_remote_copy(
            src_ref=src,
            dst_ref=dst,
            send_sem=send,
            recv_sem=recv,
            device_id=peer,
            device_id_type=MESH,
        )

    def za_copy(s, d, hop, part):
        source, target = route(s, d, hop)
        src = sa.at[part, target] if hop == 1 else ta.at[s, hop - 2, d - 2, part]
        dst = (
            za.at[part, source % ZL * ZH + source // ZL]
            if hop == d
            else ta.at[s, hop - 1, d - 2, part]
        )
        at = (s, hop - 1, d - 1, part)
        return remote(src, dst, za_send.at[at], za_recv.at[at], beside[0][s])

    def zb_copy(s, d, hop):
        source, target = route(s, d, hop)
        at = pl.ds(s * (NX // 2), NX // 2) if d == FAR else pl.ds(0, NX)
        src = yb.at[at, :, target] if hop == 1 else tb.at[s, hop - 2, d - 2, at]
        dst = (
            rb.at[source % ZL, at, :, source // ZL]
            if hop == d
            else tb.at[s, hop - 1, d - 2, at]
        )
        at = (s, hop - 1, d - 1)
        return remote(src, dst, zb_send.at[at], zb_recv.at[at], beside[0][s])

    stage, rings, passing = (ca, cb), (xa, xb), (via0, via1)
    per = NZ // 2

    def core_copy(half, src):
        return remote(
            src.at[1 - c], stage[half].at[:, c], core_send.at[half], core_recv.at[half], twin
        )

    def own_core(half, src):
        return pltpu.make_async_copy(
            src.at[c], stage[half].at[:, c], local_sem.at[half, 0]
        )

    def leg_src(half, unit, leg, to, lo, n):
        along_x = unit == leg
        if leg == 1:
            return rings[half].at[unit, :, pl.ds(lo, n), :, to]
        at = pl.ds(unit * per + lo, n)
        return stage[half].at[at, :, :, to] if along_x else stage[half].at[at, :, to]

    def leg_dst(half, unit, leg, frm, lo, n):
        along_x = unit == leg
        if leg == 0:
            return rings[half].at[unit, frm, pl.ds(lo, n)]
        if half == 0:
            at = pl.ds(lo, n)
            if along_x:
                return ra.at[unit, frm, :, at]
            return ra.at[unit, :, frm, at]
        at = pl.ds(unit * per + lo, n)
        return yb.at[frm, :, at] if along_x else yb.at[:, frm, at]

    def plane_copy(half, unit, leg, s, kind):
        along_x = unit == leg
        size, mine = (NX, x) if along_x else (NY, y)
        sign = 1 - 2 * s
        lo, n = (0, per) if kind == 0 else (s * per // 2, per // 2)
        peer = beside[1 if along_x else 2][s]
        via = passing[leg].at[half, unit, s]
        if kind == 0:
            src = leg_src(half, unit, leg, (mine + size + sign) % size, lo, n)
            dst = leg_dst(half, unit, leg, mine, lo, n)
        elif kind == 1:
            src = leg_src(half, unit, leg, (mine + 2) % size, lo, n)
            dst = via
        else:
            src = via
            dst = leg_dst(half, unit, leg, (mine + size - sign) % size, lo, n)
        at = (half, unit, leg, s, kind)
        return remote(src, dst, plane_send.at[at], plane_recv.at[at], peer)

    def own_leg(half, unit, leg):
        mine = x if unit == leg else y
        return pltpu.make_async_copy(
            leg_src(half, unit, leg, mine, 0, per),
            leg_dst(half, unit, leg, mine, 0, per),
            local_sem.at[half, 1 + 2 * unit + leg],
        )

    every_leg = [(unit, s) for unit in range(2) for s in range(2)]

    def legs_start(half, leg, first=False):
        for s in range(2):
            if first and s == 1:
                pl.semaphore_wait(ready.at[1], 1)
                pl.semaphore_wait(ready.at[2], 1)
            for kind in (1, 0):
                for unit in range(2):
                    plane_copy(half, unit, leg, s, kind).start()
        for unit in range(2):
            own_leg(half, unit, leg).start()

    def legs_forward(half, leg):
        for unit, s in every_leg:
            plane_copy(half, unit, leg, s, 1).wait_recv()
            plane_copy(half, unit, leg, s, 2).start()

    def legs_wait(half, leg):
        for unit, s in every_leg:
            plane_copy(half, unit, leg, s, 0).wait_recv()
            plane_copy(half, unit, leg, s, 2).wait_recv()
        for unit in range(2):
            own_leg(half, unit, leg).wait()

    def za_forward(hop):
        for d in range(FAR, hop - 1, -1):
            for s, p in legs_a(d):
                za_copy(s, d, hop - 1, p).wait_recv()
                za_copy(s, d, hop, p).start()

    def zb_forward(hop):
        for d in range(FAR, hop - 1, -1):
            for s in range(2):
                zb_copy(s, d, hop - 1).wait_recv()
                zb_copy(s, d, hop).start()

    def legs_a(d):
        return [(s, part) for part in range(2) for s in range(2) if d < FAR or s == part]

    load(middle - 1).wait()
    filter_pieces(middle, PIECES, True)
    load_table.wait()

    for part in range(NC):
        transform(0, part, sa)
        for s in range(2):
            if part == 0 and s == 1:
                pl.semaphore_wait(ready.at[0], 1)
            for d in range(FAR, 0, -1):
                if (s, part) in legs_a(d):
                    za_copy(s, d, 1, part).start()
    keep_a = pltpu.make_async_copy(sa.at[:, z], za.at[:, zl * ZH + zh], local_sem.at[0, 5])
    keep_a.start()

    for g in range(middle - 1):
        load(g).wait()
    filter_pieces(0, middle, False)
    first_spectra()
    for part in range(NC):
        transform(1, part, sb)
    core_copy(1, sb).start()
    own_core(1, sb).start()
    core_copy(1, sb).wait()
    own_core(1, sb).wait()
    legs_start(1, 0, first=True)
    za_forward(2)
    legs_forward(1, 0)
    legs_wait(1, 0)
    legs_start(1, 1)
    za_forward(3)
    legs_forward(1, 1)
    za_forward(4)
    legs_wait(1, 1)

    for d in range(FAR, 0, -1):
        for s in range(2):
            zb_copy(s, d, 1).start()
    last_b = pltpu.make_async_copy(
        yb.at[:, :, z], rb.at[zl, :, :, zh], local_sem.at[1, 5]
    )
    last_b.start()

    for d in range(1, FAR + 1):
        for s, p in legs_a(d):
            za_copy(s, d, d, p).wait_recv()
    keep_a.wait()
    core_copy(0, za).start()
    own_core(0, za).start()
    core_copy(0, za).wait()
    own_core(0, za).wait()
    legs_start(0, 0)
    zb_forward(2)
    legs_forward(0, 0)
    legs_wait(0, 0)
    legs_start(0, 1)
    zb_forward(3)
    legs_forward(0, 1)
    zb_forward(4)

    legs_wait(0, 1)
    for plane, low, value in products(ra):
        if low:
            sums[plane, cut:, cut:] = value
        else:
            sums[plane, :cut, :] = value
    for d in range(1, FAR + 1):
        for hop in range(1, d + 1):
            for s, p in legs_a(d):
                za_copy(s, d, hop, p).wait_send()
    for half in (1, 0):
        for leg in range(2):
            for unit, s in every_leg:
                for kind in range(3):
                    plane_copy(half, unit, leg, s, kind).wait_send()
    last_b.wait()
    for d in range(1, FAR + 1):
        for s in range(2):
            zb_copy(s, d, d).wait_recv()
    for d in range(1, FAR + 1):
        for hop in range(1, d + 1):
            for s in range(2):
                zb_copy(s, d, hop).wait_send()


def exchange(voltages, taps, table):
    rows, samples = voltages.shape
    width = taps.shape[1]
    inputs = rows * lax.axis_size("inp")
    block = (rows, LANES)
    bf16, f32 = jnp.bfloat16, jnp.float32
    dma = pltpu.SemaphoreType.DMA
    vmem = pltpu.VMEM
    operands = [
        pltpu.with_memory_space_constraint(a, pltpu.HBM) for a in (voltages, taps, table)
    ]
    gathered = (ZL, NX, NY, ZH, NC) + block
    return pl.pallas_call(
        exchange_kernel,
        name="exchange",
        out_shape=(
            jax.ShapeDtypeStruct(gathered, bf16),
            jax.ShapeDtypeStruct((2, inputs, inputs), f32),
        ),
        in_specs=[pl.BlockSpec(memory_space=pltpu.HBM)] * 3,
        out_specs=(pl.BlockSpec(memory_space=vmem),) * 2,
        scratch_shapes=[
            vmem(gathered, bf16),
            vmem((rows, samples), bf16),
            vmem(taps.shape, taps.dtype),
            vmem(table.shape, table.dtype),
            vmem((rows, (taps.shape[0] - 1) * width), bf16),
            vmem((width // LANES, rows * PITCH, LANES), f32),
            vmem((width // 2 * rows, LANES), f32),
            vmem((NC, NZ, NY, NX) + block, bf16),
            vmem((NC, NZ, NY, NX) + block, bf16),
            vmem((NC, NZ, NY, NX) + block, bf16),
            vmem((NX, NY, NZ, NC) + block, bf16),
            vmem((2, FAR - 1, FAR - 1, NC, NY, NX) + block, bf16),
            vmem((2, FAR - 1, FAR - 1, NX, NY, NC) + block, bf16),
            vmem((NZ, NC, NY, NX) + block, bf16),
            vmem((NZ, NC, NY, NX) + block, bf16),
            vmem((2, NX, NZ // 2, NC, NY) + block, bf16),
            vmem((2, NX, NZ // 2, NC, NY) + block, bf16),
            vmem((2, 2, 2, NZ // 4, NC, NY) + block, bf16),
            vmem((2, 2, 2, NX, NZ // 4, NC) + block, bf16),
            dma((PIECES + 2,)), dma(()), dma(()), dma((2, 6)),
            pltpu.SemaphoreType.REGULAR((3,)), dma((2,)), dma((2,)),
            dma((2, FAR, FAR, NC)), dma((2, FAR, FAR, NC)),
            dma((2, FAR, FAR)), dma((2, FAR, FAR)),
            dma((2, 2, 2, 2, 3)), dma((2, 2, 2, 2, 3)),
        ],
        compiler_params=pltpu.CompilerParams(
            collective_id=0, has_side_effects=True, vmem_limit_bytes=48 << 20
        ),
    )(*operands)


def correlate_kernel(scale, r_ref, sums, o_hbm, o, sem):
    cut = sums.shape[1] // 2
    copies = []

    def put(plane, part):
        at = pl.ds(part * cut, cut)
        copy = pltpu.make_async_copy(
            o.at[plane, at], o_hbm.at[0, plane, at], sem.at[2 * plane + part]
        )
        copy.start()
        copies.append(copy)

    for plane, low, value in products(r_ref):
        if low:
            o[plane, cut:, cut:] = (sums[plane, cut:, cut:] + value) * scale
        else:
            top = (sums[plane, :cut, :] + value) * scale
            o[plane, :cut, :] = top
            corner = top[:, cut:].T
            o[plane, cut:, :cut] = -corner if plane else corner
        put(plane, int(low))
    for copy in copies:
        copy.wait()


def correlate(spectra, sums, scale):
    inputs = sums.shape[1]
    return pl.pallas_call(
        functools.partial(correlate_kernel, scale),
        name="correlate",
        out_shape=jax.ShapeDtypeStruct((1, 2, inputs, inputs), jnp.float32),
        in_specs=[pl.BlockSpec(memory_space=pltpu.VMEM)] * 2,
        out_specs=pl.BlockSpec(memory_space=pltpu.HBM),
        scratch_shapes=[
            pltpu.VMEM((2, inputs, inputs), jnp.float32),
            pltpu.SemaphoreType.DMA((4,)),
        ],
        compiler_params=pltpu.CompilerParams(vmem_limit_bytes=32 << 20),
    )(spectra, sums)


def local(voltages, taps):
    width = taps.shape[1]
    table = jnp.asarray(dft_rows(width))
    scale = 1.0 / (voltages.shape[1] * lax.axis_size("tm"))
    return correlate(*exchange(voltages, taps, table), scale)


def solution(mesh):
    in_specs = (P("inp", "tm"), P())
    out_specs = P(("inp", "tm"), None, None, None)
    return jax.shard_map(local, mesh=mesh, in_specs=in_specs, out_specs=out_specs, check_vma=False)
```

```python
import functools
import math

import jax
import jax.numpy as jnp
import ml_dtypes
import numpy as np
from jax import lax
from jax.experimental import pallas as pl
from jax.experimental.pallas import tpu as pltpu
from jax.sharding import PartitionSpec as P

MESH = pl.DeviceIdType.MESH
NX, NY, NZ, NC, ZL = 4, 4, 8, 2, 2
ZH = NZ // ZL
PLANE = NY * NX * NC
FAR = NZ // 2
LANES = 128
PIECES = 8
PITCH = 136


def position():
    inp = lax.axis_index("inp")
    tm = lax.axis_index("tm")
    return tm % NX, inp // (ZH * NC), (inp // NC) % ZH * ZL + tm // NX, inp % NC


def device(x, y, z, c):
    return (y * ZH + z // ZL) * NC + c, (z % ZL) * NX + x


def channel_of_row():
    order = np.empty((NC, NZ, NY, NX), np.int64)
    for c in range(NC):
        for z in range(NZ):
            for y in range(NY):
                for x in range(NX):
                    inp, tm = device(x, y, z, c)
                    order[c, z, y, x] = inp * (ZL * NX) + tm
    return order.reshape(-1)


def dft_rows(width):
    parts = []
    for channel in np.split(channel_of_row(), NC):
        phase = (channel[:, None] * np.arange(width)[None, :]) % width
        angle = phase.astype(np.float32) * np.float32(2.0 * math.pi / width)
        parts += [np.cos(angle), -np.sin(angle)]
    return np.concatenate(parts, axis=0).astype(ml_dtypes.bfloat16)


def products(times):
    inputs = math.prod(times[0].shape[:-1])
    cut = inputs // 2
    times = [t.reshape(inputs, LANES) for t in times]
    every = jnp.concatenate(times, axis=1)
    half = LANES // 2
    turned = jnp.concatenate(
        [part for t in times for part in (t[:, half:], -t[:, :half])], axis=1
    )
    for plane, left in ((0, every), (1, turned)):
        for low in (False, True):
            at = slice(cut, inputs) if low else slice(0, cut)
            yield plane, low, lax.dot_general(
                left[at],
                every[cut:] if low else every,
                (((1,), (1,)), ((), ())),
                preferred_element_type=jnp.float32,
            )


def exchange_kernel(
    v_hbm, taps_hbm, table_hbm, rb, sums, ra, rc,
    v, taps_ref, table_ref, hist, f32s, s32, sa, sb, za, yb, ta, tb, ca, cb, xa, xb, via0, via1,
    load_sem, hist_send, hist_recv, local_sem,
    ready, core_send, core_recv, za_send, za_recv, zb_send, zb_recv, plane_send, plane_recv,
):
    x, y, z, c = position()
    zh, zl = z // ZL, z % ZL
    tm = lax.axis_index("tm")
    inp = lax.axis_index("inp")
    tms = ZL * NX
    taps_n, width = taps_ref.shape
    rows = v.shape[0]
    spectra = v.shape[1] // width
    piece = spectra // PIECES
    span = spectra // 2
    tail = (taps_n - 1) * width
    count = NZ * NY * NX
    cut = sums.shape[1] // 2

    def load(g):
        at = pl.ds(pl.multiple_of(g * piece * width, width), piece * width)
        return pltpu.make_async_copy(v_hbm.at[:, at], v.at[:, at], load_sem.at[g])

    load_taps = pltpu.make_async_copy(taps_hbm, taps_ref, load_sem.at[PIECES])

    def load_table(part):
        at = pl.ds(part * 2 * count, 2 * count)
        return pltpu.make_async_copy(
            table_hbm.at[at], table_ref.at[at], load_sem.at[PIECES + 1 + part]
        )

    middle = PIECES // 2
    load_taps.start()
    for g in range(middle - 1, PIECES):
        load(g).start()
    for part in range(NC):
        load_table(part).start()
    for g in range(middle - 1):
        load(g).start()

    beside = (
        (device(x, y, (z + 1) % NZ, c), device(x, y, (z + NZ - 1) % NZ, c)),
        (device((x + 1) % NX, y, z, c), device((x + NX - 1) % NX, y, z, c)),
        (device(x, (y + 1) % NY, z, c), device(x, (y + NY - 1) % NY, z, c)),
    )
    twin = device(x, y, z, 1 - c)
    later = (inp, (tm + 1) % tms)
    earlier = (inp, (tm + tms - 1) % tms)

    barrier = pltpu.get_barrier_semaphore()
    callers = (beside[0][1], beside[1][1], beside[2][1], twin, earlier)
    for peer in callers:
        pl.semaphore_signal(barrier, inc=1, device_id=peer, device_id_type=MESH)
    pl.semaphore_wait(barrier, len(callers))
    for axis in range(3):
        pl.semaphore_signal(
            ready.at[axis], inc=1, device_id=beside[axis][0], device_id_type=MESH
        )

    history = pltpu.make_async_remote_copy(
        src_ref=v_hbm.at[:, pl.ds(spectra * width - tail, tail)],
        dst_ref=hist,
        send_sem=hist_send,
        recv_sem=hist_recv,
        device_id=later,
        device_id_type=MESH,
    )
    history.start()
    load_taps.wait()

    def block(ref, s, q):
        at = pl.multiple_of(s * width + q * LANES, LANES)
        return ref[:, pl.ds(at, LANES)].astype(jnp.float32)

    def gain(q):
        return [
            jnp.broadcast_to(taps_ref[t : t + 1, q * LANES : (q + 1) * LANES], (rows, LANES))
            for t in range(taps_n)
        ]

    def step(gains, s, q, past):
        past = past + (block(v, s, q),)
        total = gains[0] * past[0]
        for t in range(1, taps_n):
            total = total + gains[t] * past[t]
        f32s.at[q][pl.ds(s, rows, stride=PITCH), :] = total
        return past[1:]

    def filter_pieces(lo, hi, wait):
        def filter_piece(g, _):
            if wait:
                load(g).wait()
            for q in range(width // LANES):
                gains = gain(q)
                past = tuple(
                    block(v, jnp.maximum(g * piece - k, 0), q) for k in range(taps_n - 1, 0, -1)
                )
                for j in range(piece):
                    past = step(gains, g * piece + j, q, past)
            return 0

        lax.fori_loop(lo, hi, filter_piece, 0)

    def first_spectra():
        history.wait()
        for q in range(width // LANES):
            gains = gain(q)
            past = tuple(jnp.where(tm > 0, block(hist, s, q), 0.0) for s in range(taps_n - 1))
            for s in range(taps_n - 1):
                past = step(gains, s, q, past)

    def transform(half, part, out):
        first = lax.broadcasted_iota(jnp.int32, (count, LANES), 1) < span

        def filtered(i):
            at = i * PITCH + (1 - half) * span
            return jnp.concatenate(
                [f32s[q, at : at + span, :] for q in range(width // LANES)], axis=1
            ).astype(jnp.bfloat16)

        for i in range(0, rows, 4):
            spec = lax.dot_general(
                table_ref[part * 2 * count : (part + 1) * 2 * count, :],
                jnp.concatenate([filtered(i + k) for k in range(4)], axis=0),
                (((1,), (1,)), ((), ())),
                preferred_element_type=jnp.float32,
            )
            for two in range(2):
                real = spec[:count, two * LANES : (two + 1) * LANES]
                imag = spec[count:, two * LANES : (two + 1) * LANES]
                pairs = (
                    jnp.where(first, real, pltpu.roll(imag, span, 1)),
                    jnp.where(first, pltpu.roll(real, span, 1), imag),
                )
                for k in range(2):
                    at = pl.ds(part * count * rows + i + 2 * two + k, count, stride=rows)
                    s32[at, :] = pairs[k]

        def pack(m, _):
            size = NY * NX * rows
            at = pl.ds(pl.multiple_of((part * NZ + m) * size, size), size)
            out[part, m] = s32[at, :].reshape(NY, NX, rows, LANES).astype(jnp.bfloat16)
            return 0

        lax.fori_loop(0, NZ, pack, 0)

    def route(s, d, hop):
        sign = 1 - 2 * s
        source = (z + NZ - (hop - 1) * sign) % NZ
        return source, (source + NZ + d * sign) % NZ

    def remote(src, dst, send, recv, peer):
        return pltpu.make_async_remote_copy(
            src_ref=src,
            dst_ref=dst,
            send_sem=send,
            recv_sem=recv,
            device_id=peer,
            device_id_type=MESH,
        )

    def za_copy(s, d, hop, part):
        source, target = route(s, d, hop)
        src = sa.at[part, target] if hop == 1 else ta.at[s, hop - 2, d - 2, part]
        dst = (
            za.at[part, source % ZL * ZH + source // ZL]
            if hop == d
            else ta.at[s, hop - 1, d - 2, part]
        )
        at = (s, hop - 1, d - 1, part)
        return remote(src, dst, za_send.at[at], za_recv.at[at], beside[0][s])

    def zb_copy(s, d, hop):
        source, target = route(s, d, hop)
        at = pl.ds(s * (NX // 2), NX // 2) if d == FAR else pl.ds(0, NX)
        src = yb.at[at, :, target] if hop == 1 else tb.at[s, hop - 2, d - 2, at]
        dst = (
            (rb if d % ZL else rc).at[at, :, source // ZL]
            if hop == d
            else tb.at[s, hop - 1, d - 2, at]
        )
        at = (s, hop - 1, d - 1)
        return remote(src, dst, zb_send.at[at], zb_recv.at[at], beside[0][s])

    stage, rings, passing = (ca, cb), (xa, xb), (via0, via1)
    per = NZ // 2

    def core_copy(half, src):
        return remote(
            src.at[1 - c], stage[half].at[:, c], core_send.at[half], core_recv.at[half], twin
        )

    def own_core(half, src):
        return pltpu.make_async_copy(
            src.at[c], stage[half].at[:, c], local_sem.at[half, 0]
        )

    def leg_src(half, unit, leg, to, lo, n):
        along_x = unit == leg
        if leg == 1:
            return rings[half].at[unit, :, pl.ds(lo, n), :, to]
        at = pl.ds(unit * per + lo, n)
        return stage[half].at[at, :, :, to] if along_x else stage[half].at[at, :, to]

    def leg_dst(half, unit, leg, frm, lo, n):
        along_x = unit == leg
        if leg == 0:
            return rings[half].at[unit, frm, pl.ds(lo, n)]
        if half == 0:
            at = pl.ds(lo, n)
            if along_x:
                return ra.at[unit, frm, :, at]
            return ra.at[unit, :, frm, at]
        at = pl.ds(unit * per + lo, n)
        return yb.at[frm, :, at] if along_x else yb.at[:, frm, at]

    def plane_copy(half, unit, leg, s, kind):
        along_x = unit == leg
        size, mine = (NX, x) if along_x else (NY, y)
        sign = 1 - 2 * s
        lo, n = (0, per) if kind == 0 else (s * per // 2, per // 2)
        peer = beside[1 if along_x else 2][s]
        via = passing[leg].at[half, unit, s]
        if kind == 0:
            src = leg_src(half, unit, leg, (mine + size + sign) % size, lo, n)
            dst = leg_dst(half, unit, leg, mine, lo, n)
        elif kind == 1:
            src = leg_src(half, unit, leg, (mine + 2) % size, lo, n)
            dst = via
        else:
            src = via
            dst = leg_dst(half, unit, leg, (mine + size - sign) % size, lo, n)
        at = (half, unit, leg, s, kind)
        return remote(src, dst, plane_send.at[at], plane_recv.at[at], peer)

    def own_leg(half, unit, leg):
        mine = x if unit == leg else y
        return pltpu.make_async_copy(
            leg_src(half, unit, leg, mine, 0, per),
            leg_dst(half, unit, leg, mine, 0, per),
            local_sem.at[half, 1 + 2 * unit + leg],
        )

    every_leg = [(unit, s) for unit in range(2) for s in range(2)]

    def legs_start(half, leg, first=False):
        for s in range(2):
            if first and s == 1:
                pl.semaphore_wait(ready.at[1], 1)
                pl.semaphore_wait(ready.at[2], 1)
            for kind in (1, 0):
                for unit in range(2):
                    plane_copy(half, unit, leg, s, kind).start()
        for unit in range(2):
            own_leg(half, unit, leg).start()

    def legs_forward(half, leg):
        for unit, s in every_leg:
            plane_copy(half, unit, leg, s, 1).wait_recv()
            plane_copy(half, unit, leg, s, 2).start()

    def legs_wait(half, leg):
        for unit, s in every_leg:
            plane_copy(half, unit, leg, s, 0).wait_recv()
            plane_copy(half, unit, leg, s, 2).wait_recv()
        for unit in range(2):
            own_leg(half, unit, leg).wait()

    def za_forward(hop):
        for d in range(FAR, hop - 1, -1):
            for s, p in legs_a(d):
                za_copy(s, d, hop - 1, p).wait_recv()
                za_copy(s, d, hop, p).start()

    def zb_forward(hop):
        for d in range(FAR, hop - 1, -1):
            for s in range(2):
                zb_copy(s, d, hop - 1).wait_recv()
                zb_copy(s, d, hop).start()

    def legs_a(d):
        return [(s, part) for part in range(2) for s in range(2) if d < FAR or s == part]

    load(middle - 1).wait()
    filter_pieces(middle, PIECES, True)

    for part in range(NC):
        load_table(part).wait()
        transform(0, part, sa)
        for s in range(2):
            if part == 0 and s == 1:
                pl.semaphore_wait(ready.at[0], 1)
            for d in range(FAR, 0, -1):
                if (s, part) in legs_a(d):
                    za_copy(s, d, 1, part).start()
    keep_a = pltpu.make_async_copy(sa.at[:, z], za.at[:, zl * ZH + zh], local_sem.at[0, 5])
    keep_a.start()

    for g in range(middle - 1):
        load(g).wait()
    filter_pieces(0, middle, False)
    first_spectra()
    for part in range(NC):
        transform(1, part, sb)
    core_copy(1, sb).start()
    own_core(1, sb).start()
    core_copy(1, sb).wait()
    own_core(1, sb).wait()
    legs_start(1, 0, first=True)
    za_forward(2)
    legs_forward(1, 0)
    legs_wait(1, 0)
    legs_start(1, 1)
    za_forward(3)
    legs_forward(1, 1)
    za_forward(4)
    legs_wait(1, 1)

    for d in range(FAR, 1, -1):
        for s in range(2):
            zb_copy(s, d, 1).start()
    last_b = pltpu.make_async_copy(
        yb.at[:, :, z], rc.at[:, :, zh], local_sem.at[1, 5]
    )
    last_b.start()

    for d in range(1, FAR + 1):
        for s, p in legs_a(d):
            za_copy(s, d, d, p).wait_recv()
    keep_a.wait()
    core_copy(0, za).start()
    own_core(0, za).start()
    core_copy(0, za).wait()
    own_core(0, za).wait()
    legs_start(0, 0)
    zb_forward(2)
    legs_forward(0, 0)
    legs_wait(0, 0)
    legs_start(0, 1)
    zb_forward(3)
    legs_forward(0, 1)
    zb_forward(4)
    for s in range(2):
        zb_copy(s, 1, 1).start()

    legs_wait(0, 1)
    def gather(ref):
        return [ref[t] for t in range(NX)]

    for plane, low, value in products(gather(ra.at[0]) + gather(ra.at[1])):
        at = (plane, slice(cut, None), slice(cut, None)) if low else (plane, slice(0, cut))
        sums[at] = value

    for d in range(1, FAR + 1):
        for hop in range(1, d + 1):
            for s, p in legs_a(d):
                za_copy(s, d, hop, p).wait_send()
    for half in (1, 0):
        for leg in range(2):
            for unit, s in every_leg:
                for kind in range(3):
                    plane_copy(half, unit, leg, s, kind).wait_send()
    last_b.wait()
    for d in (2, 4):
        for s in range(2):
            zb_copy(s, d, d).wait_recv()
    for plane, low, value in products(gather(rc)):
        at = (plane, slice(cut, None), slice(cut, None)) if low else (plane, slice(0, cut))
        sums[at] += value
    for d in (1, 3):
        for s in range(2):
            zb_copy(s, d, d).wait_recv()
    for d in range(1, FAR + 1):
        for hop in range(1, d + 1):
            for s in range(2):
                zb_copy(s, d, hop).wait_send()


def exchange(voltages, taps, table):
    rows, samples = voltages.shape
    width = taps.shape[1]
    inputs = rows * lax.axis_size("inp")
    block = (rows, LANES)
    bf16, f32 = jnp.bfloat16, jnp.float32
    dma = pltpu.SemaphoreType.DMA
    vmem = pltpu.VMEM
    operands = [
        pltpu.with_memory_space_constraint(a, pltpu.HBM) for a in (voltages, taps, table)
    ]
    gathered = (NX, NY, ZH, NC) + block
    return pl.pallas_call(
        exchange_kernel,
        name="exchange",
        out_shape=(
            jax.ShapeDtypeStruct(gathered, bf16),
            jax.ShapeDtypeStruct((2, inputs, inputs), f32),
        ),
        in_specs=[pl.BlockSpec(memory_space=pltpu.HBM)] * 3,
        out_specs=(pl.BlockSpec(memory_space=vmem),) * 2,
        scratch_shapes=[
            vmem((ZL,) + gathered, bf16),
            vmem(gathered, bf16),
            vmem((rows, samples), bf16),
            vmem(taps.shape, taps.dtype),
            vmem(table.shape, table.dtype),
            vmem((rows, (taps.shape[0] - 1) * width), bf16),
            vmem((width // LANES, rows * PITCH, LANES), f32),
            vmem((width // 2 * rows, LANES), f32),
            vmem((NC, NZ, NY, NX) + block, bf16),
            vmem((NC, NZ, NY, NX) + block, bf16),
            vmem((NC, NZ, NY, NX) + block, bf16),
            vmem((NX, NY, NZ, NC) + block, bf16),
            vmem((2, FAR - 1, FAR - 1, NC, NY, NX) + block, bf16),
            vmem((2, FAR - 1, FAR - 1, NX, NY, NC) + block, bf16),
            vmem((NZ, NC, NY, NX) + block, bf16),
            vmem((NZ, NC, NY, NX) + block, bf16),
            vmem((2, NX, NZ // 2, NC, NY) + block, bf16),
            vmem((2, NX, NZ // 2, NC, NY) + block, bf16),
            vmem((2, 2, 2, NZ // 4, NC, NY) + block, bf16),
            vmem((2, 2, 2, NX, NZ // 4, NC) + block, bf16),
            dma((PIECES + 1 + NC,)), dma(()), dma(()), dma((2, 6)),
            pltpu.SemaphoreType.REGULAR((3,)), dma((2,)), dma((2,)),
            dma((2, FAR, FAR, NC)), dma((2, FAR, FAR, NC)),
            dma((2, FAR, FAR)), dma((2, FAR, FAR)),
            dma((2, 2, 2, 2, 3)), dma((2, 2, 2, 2, 3)),
        ],
        compiler_params=pltpu.CompilerParams(
            collective_id=0, has_side_effects=True, vmem_limit_bytes=48 << 20
        ),
    )(*operands)


def correlate_kernel(scale, r_ref, sums, o_hbm, o, sem):
    cut = sums.shape[1] // 2
    copies = []

    def put(plane, part):
        at = pl.ds(part * cut, cut)
        copy = pltpu.make_async_copy(
            o.at[plane, at], o_hbm.at[0, plane, at], sem.at[2 * plane + part]
        )
        copy.start()
        copies.append(copy)

    for plane, low, value in products([r_ref[t] for t in range(NX)]):
        if low:
            o[plane, cut:, cut:] = (sums[plane, cut:, cut:] + value) * scale
        else:
            top = (sums[plane, :cut, :] + value) * scale
            o[plane, :cut, :] = top
            corner = top[:, cut:].T
            o[plane, cut:, :cut] = -corner if plane else corner
        put(plane, int(low))
    for copy in copies:
        copy.wait()


def correlate(spectra, sums, scale):
    inputs = sums.shape[1]
    return pl.pallas_call(
        functools.partial(correlate_kernel, scale),
        name="correlate",
        out_shape=jax.ShapeDtypeStruct((1, 2, inputs, inputs), jnp.float32),
        in_specs=[pl.BlockSpec(memory_space=pltpu.VMEM)] * 2,
        out_specs=pl.BlockSpec(memory_space=pltpu.HBM),
        scratch_shapes=[
            pltpu.VMEM((2, inputs, inputs), jnp.float32),
            pltpu.SemaphoreType.DMA((4,)),
        ],
        compiler_params=pltpu.CompilerParams(vmem_limit_bytes=32 << 20),
    )(spectra, sums)


def local(voltages, taps):
    width = taps.shape[1]
    table = jnp.asarray(dft_rows(width))
    scale = 1.0 / (voltages.shape[1] * lax.axis_size("tm"))
    return correlate(*exchange(voltages, taps, table), scale)


def solution(mesh):
    in_specs = (P("inp", "tm"), P())
    out_specs = P(("inp", "tm"), None, None, None)
    return jax.shard_map(local, mesh=mesh, in_specs=in_specs, out_specs=out_specs, check_vma=False)
```

```python
import functools
import math

import jax
import jax.numpy as jnp
import ml_dtypes
import numpy as np
from jax import lax
from jax.experimental import pallas as pl
from jax.experimental.pallas import tpu as pltpu
from jax.sharding import PartitionSpec as P

MESH = pl.DeviceIdType.MESH
NX, NY, NZ, NC, ZL = 4, 4, 8, 2, 2
ZH = NZ // ZL
PLANE = NY * NX * NC
FAR = NZ // 2
LANES = 128
PIECES = 8
PITCH = 136


def position():
    inp = lax.axis_index("inp")
    tm = lax.axis_index("tm")
    return tm % NX, inp // (ZH * NC), (inp // NC) % ZH * ZL + tm // NX, inp % NC


def device(x, y, z, c):
    return (y * ZH + z // ZL) * NC + c, (z % ZL) * NX + x


def channel_of_row():
    order = np.empty((NC, NZ, NY, NX), np.int64)
    for c in range(NC):
        for z in range(NZ):
            for y in range(NY):
                for x in range(NX):
                    inp, tm = device(x, y, z, c)
                    order[c, z, y, x] = inp * (ZL * NX) + tm
    return order.reshape(-1)


def dft_rows(width):
    parts = []
    for channel in np.split(channel_of_row(), NC):
        phase = (channel[:, None] * np.arange(width)[None, :]) % width
        angle = phase.astype(np.float32) * np.float32(2.0 * math.pi / width)
        parts += [np.cos(angle), -np.sin(angle)]
    return np.concatenate(parts, axis=0).astype(ml_dtypes.bfloat16)


def products(times):
    inputs = math.prod(times[0].shape[:-1])
    cut = inputs // 2
    times = [t.reshape(inputs, LANES) for t in times]
    every = jnp.concatenate(times, axis=1)
    half = LANES // 2
    turned = jnp.concatenate(
        [part for t in times for part in (t[:, half:], -t[:, :half])], axis=1
    )
    for plane, left in ((0, every), (1, turned)):
        for low in (False, True):
            at = slice(cut, inputs) if low else slice(0, cut)
            yield plane, low, lax.dot_general(
                left[at],
                every[cut:] if low else every,
                (((1,), (1,)), ((), ())),
                preferred_element_type=jnp.float32,
            )


def exchange_kernel(
    v_hbm, taps_hbm, table_hbm, rb, sums, ra, rc,
    v, taps_ref, table_ref, hist, f32s, s32, sa, sb, za, yb, ta, tb, ca, cb, xa, xb, via0, via1,
    load_sem, hist_send, hist_recv, local_sem,
    ready, core_send, core_recv, za_send, za_recv, zb_send, zb_recv, plane_send, plane_recv,
):
    x, y, z, c = position()
    zh, zl = z // ZL, z % ZL
    tm = lax.axis_index("tm")
    inp = lax.axis_index("inp")
    tms = ZL * NX
    taps_n, width = taps_ref.shape
    rows = v.shape[0]
    spectra = v.shape[1] // width
    piece = spectra // PIECES
    span = spectra // 2
    tail = (taps_n - 1) * width
    count = NZ * NY * NX
    cut = sums.shape[1] // 2

    def load(g):
        at = pl.ds(pl.multiple_of(g * piece * width, width), piece * width)
        return pltpu.make_async_copy(v_hbm.at[:, at], v.at[:, at], load_sem.at[g])

    load_taps = pltpu.make_async_copy(taps_hbm, taps_ref, load_sem.at[PIECES])

    def load_table(part):
        at = pl.ds(part * 2 * count, 2 * count)
        return pltpu.make_async_copy(
            table_hbm.at[at], table_ref.at[at], load_sem.at[PIECES + 1 + part]
        )

    middle = PIECES // 2
    load_taps.start()
    for g in range(middle - 1, PIECES):
        load(g).start()
    for part in range(NC):
        load_table(part).start()
    for g in range(middle - 1):
        load(g).start()

    beside = (
        (device(x, y, (z + 1) % NZ, c), device(x, y, (z + NZ - 1) % NZ, c)),
        (device((x + 1) % NX, y, z, c), device((x + NX - 1) % NX, y, z, c)),
        (device(x, (y + 1) % NY, z, c), device(x, (y + NY - 1) % NY, z, c)),
    )
    twin = device(x, y, z, 1 - c)
    later = (inp, (tm + 1) % tms)
    earlier = (inp, (tm + tms - 1) % tms)

    barrier = pltpu.get_barrier_semaphore()
    callers = (beside[0][1], beside[1][1], beside[2][1], twin, earlier)
    for peer in callers:
        pl.semaphore_signal(barrier, inc=1, device_id=peer, device_id_type=MESH)
    pl.semaphore_wait(barrier, len(callers))
    for axis in range(3):
        pl.semaphore_signal(
            ready.at[axis], inc=1, device_id=beside[axis][0], device_id_type=MESH
        )

    history = pltpu.make_async_remote_copy(
        src_ref=v_hbm.at[:, pl.ds(spectra * width - tail, tail)],
        dst_ref=hist,
        send_sem=hist_send,
        recv_sem=hist_recv,
        device_id=later,
        device_id_type=MESH,
    )
    history.start()
    load_taps.wait()

    def block(ref, s, q):
        at = pl.multiple_of(s * width + q * LANES, LANES)
        return ref[:, pl.ds(at, LANES)].astype(jnp.float32)

    def gain(q):
        return [
            jnp.broadcast_to(taps_ref[t : t + 1, q * LANES : (q + 1) * LANES], (rows, LANES))
            for t in range(taps_n)
        ]

    def step(gains, s, q, past):
        past = past + (block(v, s, q),)
        total = gains[0] * past[0]
        for t in range(1, taps_n):
            total = total + gains[t] * past[t]
        f32s.at[q][pl.ds(s, rows, stride=PITCH), :] = total
        return past[1:]

    def filter_pieces(lo, hi, wait):
        def filter_piece(g, _):
            if wait:
                load(g).wait()
            for q in range(width // LANES):
                gains = gain(q)
                past = tuple(
                    block(v, jnp.maximum(g * piece - k, 0), q) for k in range(taps_n - 1, 0, -1)
                )
                for j in range(piece):
                    past = step(gains, g * piece + j, q, past)
            return 0

        lax.fori_loop(lo, hi, filter_piece, 0)

    def first_spectra():
        history.wait()
        for q in range(width // LANES):
            gains = gain(q)
            past = tuple(jnp.where(tm > 0, block(hist, s, q), 0.0) for s in range(taps_n - 1))
            for s in range(taps_n - 1):
                past = step(gains, s, q, past)

    def transform(half, part, out):
        first = lax.broadcasted_iota(jnp.int32, (count, LANES), 1) < span

        def filtered(i):
            at = i * PITCH + (1 - half) * span
            return jnp.concatenate(
                [f32s[q, at : at + span, :] for q in range(width // LANES)], axis=1
            ).astype(jnp.bfloat16)

        for i in range(0, rows, 4):
            spec = lax.dot_general(
                table_ref[part * 2 * count : (part + 1) * 2 * count, :],
                jnp.concatenate([filtered(i + k) for k in range(4)], axis=0),
                (((1,), (1,)), ((), ())),
                preferred_element_type=jnp.float32,
            )
            for two in range(2):
                real = spec[:count, two * LANES : (two + 1) * LANES]
                imag = spec[count:, two * LANES : (two + 1) * LANES]
                pairs = (
                    jnp.where(first, real, pltpu.roll(imag, span, 1)),
                    jnp.where(first, pltpu.roll(real, span, 1), imag),
                )
                for k in range(2):
                    at = pl.ds(part * count * rows + i + 2 * two + k, count, stride=rows)
                    s32[at, :] = pairs[k]

        def pack(m, _):
            size = NY * NX * rows
            at = pl.ds(pl.multiple_of((part * NZ + m) * size, size), size)
            out[part, m] = s32[at, :].reshape(NY, NX, rows, LANES).astype(jnp.bfloat16)
            return 0

        lax.fori_loop(0, NZ, pack, 0)

    def route(s, d, hop):
        sign = 1 - 2 * s
        source = (z + NZ - (hop - 1) * sign) % NZ
        return source, (source + NZ + d * sign) % NZ

    def remote(src, dst, send, recv, peer):
        return pltpu.make_async_remote_copy(
            src_ref=src,
            dst_ref=dst,
            send_sem=send,
            recv_sem=recv,
            device_id=peer,
            device_id_type=MESH,
        )

    def za_copy(s, d, hop, part):
        source, target = route(s, d, hop)
        both = part == NC
        cores = pl.ds(0, NC) if both else part
        src = sa.at[cores, target] if hop == 1 else ta.at[s, hop - 2, d - 2, cores]
        dst = (
            za.at[cores, source % ZL * ZH + source // ZL]
            if hop == d
            else ta.at[s, hop - 1, d - 2, cores]
        )
        at = (s, hop - 1, d - 1)
        return remote(src, dst, za_send.at[at], za_recv.at[at], beside[0][s])

    def zb_copy(s, d, hop):
        source, target = route(s, d, hop)
        at = pl.ds(s * (NX // 2), NX // 2) if d == FAR else pl.ds(0, NX)
        src = yb.at[at, :, target] if hop == 1 else tb.at[s, hop - 2, d - 2, at]
        dst = (
            (rb if d % ZL else rc).at[at, :, source // ZL]
            if hop == d
            else tb.at[s, hop - 1, d - 2, at]
        )
        at = (s, hop - 1, d - 1)
        return remote(src, dst, zb_send.at[at], zb_recv.at[at], beside[0][s])

    stage, rings, passing = (ca, cb), (xa, xb), (via0, via1)
    per = NZ // 2

    def core_copy(half, src):
        return remote(
            src.at[1 - c], stage[half].at[:, c], core_send.at[half], core_recv.at[half], twin
        )

    def own_core(half, src):
        return pltpu.make_async_copy(
            src.at[c], stage[half].at[:, c], local_sem.at[half, 0]
        )

    def leg_src(half, unit, leg, to, lo, n):
        along_x = unit == leg
        if leg == 1:
            return rings[half].at[unit, :, pl.ds(lo, n), :, to]
        at = pl.ds(unit * per + lo, n)
        return stage[half].at[at, :, :, to] if along_x else stage[half].at[at, :, to]

    def leg_dst(half, unit, leg, frm, lo, n):
        along_x = unit == leg
        if leg == 0:
            return rings[half].at[unit, frm, pl.ds(lo, n)]
        if half == 0:
            at = pl.ds(lo, n)
            if along_x:
                return ra.at[unit, frm, :, at]
            return ra.at[unit, :, frm, at]
        at = pl.ds(unit * per + lo, n)
        return yb.at[frm, :, at] if along_x else yb.at[:, frm, at]

    def plane_copy(half, unit, leg, s, kind):
        along_x = unit == leg
        size, mine = (NX, x) if along_x else (NY, y)
        sign = 1 - 2 * s
        lo, n = (0, per) if kind == 0 else (s * per // 2, per // 2)
        peer = beside[1 if along_x else 2][s]
        via = passing[leg].at[half, unit, s]
        if kind == 0:
            src = leg_src(half, unit, leg, (mine + size + sign) % size, lo, n)
            dst = leg_dst(half, unit, leg, mine, lo, n)
        elif kind == 1:
            src = leg_src(half, unit, leg, (mine + 2) % size, lo, n)
            dst = via
        else:
            src = via
            dst = leg_dst(half, unit, leg, (mine + size - sign) % size, lo, n)
        at = (half, unit, leg, s, kind)
        return remote(src, dst, plane_send.at[at], plane_recv.at[at], peer)

    def own_leg(half, unit, leg):
        mine = x if unit == leg else y
        return pltpu.make_async_copy(
            leg_src(half, unit, leg, mine, 0, per),
            leg_dst(half, unit, leg, mine, 0, per),
            local_sem.at[half, 1 + 2 * unit + leg],
        )

    every_leg = [(unit, s) for unit in range(2) for s in range(2)]

    def legs_start(half, leg, first=False):
        for s in range(2):
            if first and s == 1:
                pl.semaphore_wait(ready.at[1], 1)
                pl.semaphore_wait(ready.at[2], 1)
            for kind in (1, 0):
                for unit in range(2):
                    plane_copy(half, unit, leg, s, kind).start()
        for unit in range(2):
            own_leg(half, unit, leg).start()

    def legs_forward(half, leg):
        for unit, s in every_leg:
            plane_copy(half, unit, leg, s, 1).wait_recv()
            plane_copy(half, unit, leg, s, 2).start()

    def legs_wait(half, leg):
        for unit, s in every_leg:
            plane_copy(half, unit, leg, s, 0).wait_recv()
            plane_copy(half, unit, leg, s, 2).wait_recv()
        for unit in range(2):
            own_leg(half, unit, leg).wait()

    def za_forward(hop, high=FAR, low=0):
        for d in range(high, max(low, hop) - 1, -1):
            for s, p in legs_a(d):
                za_copy(s, d, hop - 1, p).wait_recv()
                za_copy(s, d, hop, p).start()

    def zb_forward(hop):
        for d in range(FAR, hop - 1, -1):
            for s in range(2):
                zb_copy(s, d, hop - 1).wait_recv()
                zb_copy(s, d, hop).start()

    def legs_a(d):
        return [(s, s if d == FAR else NC) for s in range(2)]

    load(middle - 1).wait()
    filter_pieces(middle, PIECES, True)

    for part in range(NC):
        load_table(part).wait()
        transform(0, part, sa)
    pl.semaphore_wait(ready.at[0], 1)
    for d in range(FAR, 0, -1):
        for s, part in legs_a(d):
            za_copy(s, d, 1, part).start()
    keep_a = pltpu.make_async_copy(sa.at[:, z], za.at[:, zl * ZH + zh], local_sem.at[0, 5])
    keep_a.start()

    for g in range(middle - 1):
        load(g).wait()
    filter_pieces(0, middle, False)
    first_spectra()
    for part in range(NC):
        transform(1, part, sb)
    core_copy(1, sb).start()
    own_core(1, sb).start()
    core_copy(1, sb).wait()
    own_core(1, sb).wait()
    legs_start(1, 0, first=True)
    za_forward(2, FAR, 3)
    legs_forward(1, 0)
    za_forward(2, 2)
    legs_wait(1, 0)
    legs_start(1, 1)
    za_forward(3, FAR, FAR)
    legs_forward(1, 1)
    za_forward(3, FAR - 1)
    za_forward(4)
    legs_wait(1, 1)

    for d in range(FAR, 1, -1):
        for s in range(2):
            zb_copy(s, d, 1).start()
    last_b = pltpu.make_async_copy(
        yb.at[:, :, z], rc.at[:, :, zh], local_sem.at[1, 5]
    )
    last_b.start()

    for d in range(1, FAR + 1):
        for s, p in legs_a(d):
            za_copy(s, d, d, p).wait_recv()
    keep_a.wait()
    core_copy(0, za).start()
    own_core(0, za).start()
    core_copy(0, za).wait()
    own_core(0, za).wait()
    legs_start(0, 0)
    zb_forward(2)
    legs_forward(0, 0)
    legs_wait(0, 0)
    legs_start(0, 1)
    zb_forward(3)
    legs_forward(0, 1)
    zb_forward(4)
    for s in range(2):
        zb_copy(s, 1, 1).start()

    legs_wait(0, 1)
    def gather(ref):
        return [ref[t] for t in range(NX)]

    for plane, low, value in products(gather(ra.at[0]) + gather(ra.at[1])):
        at = (plane, slice(cut, None), slice(cut, None)) if low else (plane, slice(0, cut))
        sums[at] = value

    for d in range(1, FAR + 1):
        for hop in range(1, d + 1):
            for s, p in legs_a(d):
                za_copy(s, d, hop, p).wait_send()
    for half in (1, 0):
        for leg in range(2):
            for unit, s in every_leg:
                for kind in range(3):
                    plane_copy(half, unit, leg, s, kind).wait_send()
    last_b.wait()
    for d in (2, 4):
        for s in range(2):
            zb_copy(s, d, d).wait_recv()
    for plane, low, value in products(gather(rc)):
        at = (plane, slice(cut, None), slice(cut, None)) if low else (plane, slice(0, cut))
        sums[at] += value
    for d in (1, 3):
        for s in range(2):
            zb_copy(s, d, d).wait_recv()
    for d in range(1, FAR + 1):
        for hop in range(1, d + 1):
            for s in range(2):
                zb_copy(s, d, hop).wait_send()


def exchange(voltages, taps, table):
    rows, samples = voltages.shape
    width = taps.shape[1]
    inputs = rows * lax.axis_size("inp")
    block = (rows, LANES)
    bf16, f32 = jnp.bfloat16, jnp.float32
    dma = pltpu.SemaphoreType.DMA
    vmem = pltpu.VMEM
    operands = [
        pltpu.with_memory_space_constraint(a, pltpu.HBM) for a in (voltages, taps, table)
    ]
    gathered = (NX, NY, ZH, NC) + block
    return pl.pallas_call(
        exchange_kernel,
        name="exchange",
        out_shape=(
            jax.ShapeDtypeStruct(gathered, bf16),
            jax.ShapeDtypeStruct((2, inputs, inputs), f32),
        ),
        in_specs=[pl.BlockSpec(memory_space=pltpu.HBM)] * 3,
        out_specs=(pl.BlockSpec(memory_space=vmem),) * 2,
        scratch_shapes=[
            vmem((ZL,) + gathered, bf16),
            vmem(gathered, bf16),
            vmem((rows, samples), bf16),
            vmem(taps.shape, taps.dtype),
            vmem(table.shape, table.dtype),
            vmem((rows, (taps.shape[0] - 1) * width), bf16),
            vmem((width // LANES, rows * PITCH, LANES), f32),
            vmem((width // 2 * rows, LANES), f32),
            vmem((NC, NZ, NY, NX) + block, bf16),
            vmem((NC, NZ, NY, NX) + block, bf16),
            vmem((NC, NZ, NY, NX) + block, bf16),
            vmem((NX, NY, NZ, NC) + block, bf16),
            vmem((2, FAR - 1, FAR - 1, NC, NY, NX) + block, bf16),
            vmem((2, FAR - 1, FAR - 1, NX, NY, NC) + block, bf16),
            vmem((NZ, NC, NY, NX) + block, bf16),
            vmem((NZ, NC, NY, NX) + block, bf16),
            vmem((2, NX, NZ // 2, NC, NY) + block, bf16),
            vmem((2, NX, NZ // 2, NC, NY) + block, bf16),
            vmem((2, 2, 2, NZ // 4, NC, NY) + block, bf16),
            vmem((2, 2, 2, NX, NZ // 4, NC) + block, bf16),
            dma((PIECES + 1 + NC,)), dma(()), dma(()), dma((2, 6)),
            pltpu.SemaphoreType.REGULAR((3,)), dma((2,)), dma((2,)),
            dma((2, FAR, FAR)), dma((2, FAR, FAR)),
            dma((2, FAR, FAR)), dma((2, FAR, FAR)),
            dma((2, 2, 2, 2, 3)), dma((2, 2, 2, 2, 3)),
        ],
        compiler_params=pltpu.CompilerParams(
            collective_id=0, has_side_effects=True, vmem_limit_bytes=48 << 20
        ),
    )(*operands)


def correlate_kernel(scale, r_ref, sums, o_hbm, o, sem):
    cut = sums.shape[1] // 2
    copies = []

    def put(plane, part):
        at = pl.ds(part * cut, cut)
        copy = pltpu.make_async_copy(
            o.at[plane, at], o_hbm.at[0, plane, at], sem.at[2 * plane + part]
        )
        copy.start()
        copies.append(copy)

    for plane, low, value in products([r_ref[t] for t in range(NX)]):
        if low:
            o[plane, cut:, cut:] = (sums[plane, cut:, cut:] + value) * scale
        else:
            top = (sums[plane, :cut, :] + value) * scale
            o[plane, :cut, :] = top
            corner = top[:, cut:].T
            o[plane, cut:, :cut] = -corner if plane else corner
        put(plane, int(low))
    for copy in copies:
        copy.wait()


def correlate(spectra, sums, scale):
    inputs = sums.shape[1]
    return pl.pallas_call(
        functools.partial(correlate_kernel, scale),
        name="correlate",
        out_shape=jax.ShapeDtypeStruct((1, 2, inputs, inputs), jnp.float32),
        in_specs=[pl.BlockSpec(memory_space=pltpu.VMEM)] * 2,
        out_specs=pl.BlockSpec(memory_space=pltpu.HBM),
        scratch_shapes=[
            pltpu.VMEM((2, inputs, inputs), jnp.float32),
            pltpu.SemaphoreType.DMA((4,)),
        ],
        compiler_params=pltpu.CompilerParams(vmem_limit_bytes=32 << 20),
    )(spectra, sums)


def local(voltages, taps):
    width = taps.shape[1]
    table = jnp.asarray(dft_rows(width))
    scale = 1.0 / (voltages.shape[1] * lax.axis_size("tm"))
    return correlate(*exchange(voltages, taps, table), scale)


def solution(mesh):
    in_specs = (P("inp", "tm"), P())
    out_specs = P(("inp", "tm"), None, None, None)
    return jax.shard_map(local, mesh=mesh, in_specs=in_specs, out_specs=out_specs, check_vma=False)
```
